256 devices in a mesh: gz: 16 (over y, x), gx: 2 (over core), gy: 8 (over z).
Axes of the slice: x: 4, y: 4, z: 8, core: 2. Of those that a mesh axis runs over, the one named last changes fastest.
Arguments:
- conserved: float32 [5, 64, 128, 2048], P(None, 'gz', 'gx', 'gy'), may hold values from -14 to 34, as said below
- residual: float32 [5, 64, 128, 2048], P(None, 'gz', 'gx', 'gy'), may hold values from -6 to 6
Outputs:
- update: float32 [5, 64, 128, 2048], P(None, 'gz', 'gx', 'gy')
The draws below stay inside these ranges and needn't reach their ends.
Inputs may be any that keep to these rules, and one draw needn't show every extreme that they name: `conserved`: every cell has density between 0.3 and 3 and positive pressure.
All inputs are finite; a program needn't handle non-finite values.
Results may differ from the reference program's by a relative error of at most 0.0003.
Values sent between devices are 32-bit elements; how exact they have to be, the bound alone decides.
A program may use at most 192 MiB of HBM per device.

```python
import jax
import jax.numpy as jnp
from jax import lax

NX = 128
NY = 2048
DEPTH_PLANES = 64


def draw_conserved(key, part):
    random_key_list = jax.random.split(jax.random.fold_in(key, 11), 9)
    array_extent = (DEPTH_PLANES, NX, NY)
    column = (1, NX, NY)
    density = jnp.exp(jax.random.uniform(random_key_list[0], array_extent, jnp.float32, jnp.log(0.5), jnp.log(2.0)))
    speed_amplitude = jnp.exp(jax.random.uniform(random_key_list[1], column, jnp.float32, jnp.log(0.4), jnp.log(4.0)))
    spanning_count = jnp.exp(jax.random.uniform(random_key_list[2], column, jnp.float32, jnp.log(0.05), jnp.log(1.0)))
    pressure = jnp.exp(jax.random.uniform(random_key_list[3], array_extent, jnp.float32, jnp.log(0.03), jnp.log(0.12)))
    flow_bearing = jnp.where(jax.random.bernoulli(random_key_list[4], 0.5, column), 1.0, -1.0).astype(jnp.float32)
    selected_option = jax.random.randint(random_key_list[5], (3,), 0, DEPTH_PLANES)
    random_surge = jnp.any(jnp.arange(DEPTH_PLANES)[:, None] == selected_option[None, :], axis=1).astype(jnp.float32)[:, None, None]
    random_wobble = jax.random.uniform(random_key_list[6], array_extent, jnp.float32, 0.85, 1.15)
    velocity_along_z = flow_bearing * speed_amplitude * random_wobble * (1.0 - 0.9 * random_surge)
    velocity_along_x = spanning_count * (1.0 + random_surge) * jax.random.uniform(random_key_list[7], array_extent, jnp.float32, -1.0, 1.0)
    velocity_along_y = spanning_count * (1.0 + random_surge) * jax.random.uniform(random_key_list[8], array_extent, jnp.float32, -1.0, 1.0)
    energy = pressure / 0.4 + 0.5 * density * (velocity_along_x * velocity_along_x + velocity_along_y * velocity_along_y + velocity_along_z * velocity_along_z)
    return jnp.stack([density, density * velocity_along_x, density * velocity_along_y, density * velocity_along_z, energy]).astype(jnp.float32)


def block_scale(rng, extent, shards, least, largest):
    factor_of = 1.0
    for dim, blocks in shards:
        steps = jax.random.uniform(jax.random.fold_in(jax.random.fold_in(rng, 6), dim), (blocks,), jnp.float32, least / len(shards), largest / len(shards))
        factor_of = factor_of * jnp.repeat(jnp.exp(steps), extent[dim] // blocks).reshape((-1,) + (1,) * (len(extent) - 1 - dim))
    return factor_of


def gaussian(own_key, dims, spread, reach, pieces=(), dtype=jnp.bfloat16):
    entries = jax.random.normal(own_key, dims, jnp.float32) * spread
    if len(pieces) > 0:
        entries = block_scale(own_key, dims, pieces, -0.22, 0.18) * entries
    return jnp.clip(entries, min=-reach, max=reach).astype(dtype)


def setup_inputs(seed: int = 0) -> dict:
    seeds = jax.random.split(jax.random.key(seed), 3)
    return {
        "conserved": draw_conserved(jax.random.fold_in(seeds[2], 71), 0),
        "residual": gaussian(seeds[1], (5, DEPTH_PLANES, NX, NY), 1.0, 6.0, ((1, 16), (2, 2), (3, 8)), jnp.float32),
    }


ADIABATIC = 1.4
COUPLING = 0.7
METRIC = (0.1, 0.1, 1.0)

def primitives(state_field):
    density = state_field[0]
    velocity = [state_field[1] / density, state_field[2] / density, state_field[3] / density]
    kinetic = 0.5 * density * (velocity[0] * velocity[0] + velocity[1] * velocity[1] + velocity[2] * velocity[2])
    pressure = (ADIABATIC - 1.0) * (state_field[4] - kinetic)
    sound = jnp.sqrt(ADIABATIC * pressure / density)
    return (velocity, sound)

def split_jacobian(speed_dir, sound, vector, direction, upwind):
    component = 1 + direction
    radius = jnp.abs(speed_dir) + sound
    eigen = speed_dir + radius if upwind else speed_dir - radius
    zeros = jnp.zeros_like(vector[0])
    parts = [zeros, zeros, zeros, zeros, zeros]
    parts[0] = vector[component]
    parts[component] = vector[0] + vector[4]
    parts[4] = vector[component]
    coupled = jnp.stack(parts)
    return 0.5 * METRIC[direction] * (eigen * vector + COUPLING * sound * coupled)

def diagonal_of(velocity, sound):
    return METRIC[0] * (jnp.abs(velocity[0]) + sound) + METRIC[1] * (jnp.abs(velocity[1]) + sound) + METRIC[2] * (jnp.abs(velocity[2]) + sound)

def shift_lower(field, mesh_axis_name):
    widths = [(0, 0)] * field.ndim
    widths[mesh_axis_name] = (1, 0)
    return lax.slice_in_dim(jnp.pad(field, widths), 0, field.shape[mesh_axis_name], axis=mesh_axis_name)

def shift_upper(field, mesh_axis_name):
    widths = [(0, 0)] * field.ndim
    widths[mesh_axis_name] = (0, 1)
    return lax.slice_in_dim(jnp.pad(field, widths), 1, field.shape[mesh_axis_name] + 1, axis=mesh_axis_name)

def reference(conserved, residual):
    velocity, sound = primitives(conserved)
    diagonal = diagonal_of(velocity, sound)
    predictor = -residual / diagonal
    lower_x = shift_lower(split_jacobian(velocity[0], sound, predictor, 0, True), 2)
    lower_y = shift_lower(split_jacobian(velocity[1], sound, predictor, 1, True), 3)
    base = -residual + lower_x + lower_y
    upper_x = shift_upper(split_jacobian(velocity[0], sound, predictor, 0, False), 2)
    upper_y = shift_upper(split_jacobian(velocity[1], sound, predictor, 1, False), 3)
    upper_side = upper_x + upper_y

    def lower_step(carry, inputs):
        base_k, diag_k, speed_k, sound_k = inputs
        star = (base_k + carry) / diag_k
        return (split_jacobian(speed_k, sound_k, star, 2, True), star)
    initial = jnp.zeros((5, residual.shape[2], residual.shape[3]), jnp.float32)
    unused, stars = lax.scan(lower_step, initial, (jnp.moveaxis(base, 1, 0), diagonal, velocity[2], sound))
    star_field = jnp.moveaxis(stars, 0, 1)
    top = star_field - upper_side / diagonal

    def upper_step(carry, inputs):
        top_k, diag_k, speed_k, sound_k = inputs
        value = top_k - carry / diag_k
        return (split_jacobian(speed_k, sound_k, value, 2, False), value)
    unused, values = lax.scan(upper_step, initial, (jnp.moveaxis(top, 1, 0), diagonal, velocity[2], sound), reverse=True)
    return jnp.moveaxis(values, 0, 1)
```

```python
import functools
import math

import jax
import jax.numpy as jnp
from jax import lax
from jax.experimental import pallas as pl
from jax.experimental.pallas import tpu as pltpu
from jax.sharding import PartitionSpec as P

MESH = pl.DeviceIdType.MESH
ROOT2 = math.sqrt(2.0)
ADIABATIC = 1.4
COUPLING = 0.7
METRIC = (0.1, 0.1, 1.0)
CLASS = (0, 1, 2, 2, 2)
DEPTH = 4
NCOEF = 9
NTERM = 10


def tile_of(value, half):
    return value[:, 128 * half : 128 * (half + 1)]


def sweep_kernel(
    sections, gy_count, blocks,
    cons_hbm, res_hbm, out_hbm,
    cons, res, gain, base_part, up_part, faces, pull, part, scale,
    coef_out, coef_in, term_out, term_in, link_out, link_in,
    ys, yr, result,
    load_sem, coef_ssem, coef_rsem, term_ssem, term_rsem, link_ssem, link_rsem,
    halo_ssem, halo_rsem, store_sem,
):
    me = lax.axis_index("gz")
    gx = lax.axis_index("gx")
    gy = lax.axis_index("gy")
    above = lax.rem(gy + 1, gy_count)
    below = lax.rem(gy + gy_count - 1, gy_count)

    def first_block(step):
        return lax.rem(me // 2 + step, blocks)

    def loads(step):
        rows = pl.ds(pl.multiple_of(8 * first_block(step), 8), 8)
        return (
            pltpu.make_async_copy(cons_hbm.at[:, :, rows, :], cons.at[:, :, rows, :], load_sem.at[0, step]),
            pltpu.make_async_copy(res_hbm.at[:, :, rows, :], res.at[:, :, rows, :], load_sem.at[1, step]),
        )

    def start_load(step, carry):
        for copy in loads(step):
            copy.start()
        return carry

    lax.fori_loop(0, blocks, start_load, 0)

    barrier = pltpu.get_barrier_semaphore()

    def greet(step, carry):
        pl.semaphore_signal(
            barrier, inc=1, device_id={"gz": lax.rem(me + step, sections)}, device_id_type=MESH
        )
        return carry

    lax.fori_loop(1, sections, greet, 0)
    pl.semaphore_signal(barrier, inc=1, device_id={"gx": 1 - gx}, device_id_type=MESH)
    pl.semaphore_signal(barrier, inc=1, device_id={"gy": above}, device_id_type=MESH)
    pl.semaphore_signal(barrier, inc=1, device_id={"gy": below}, device_id_type=MESH)

    lane = lax.broadcasted_iota(jnp.int32, (8, 256), 1)
    sublane = lax.broadcasted_iota(jnp.int32, (8, 256), 0)
    small_lane = lax.broadcasted_iota(jnp.int32, (8, 128), 1)

    def coef_copy(tile, slot):
        return pltpu.make_async_remote_copy(
            src_ref=coef_out.at[tile], dst_ref=coef_in.at[slot],
            send_sem=coef_ssem.at[tile], recv_sem=coef_rsem.at[slot],
            device_id={"gz": tile}, device_id_type=MESH,
        )

    def term_copy(tile, slot):
        return pltpu.make_async_remote_copy(
            src_ref=term_out.at[tile], dst_ref=term_in.at[slot],
            send_sem=term_ssem.at[tile], recv_sem=term_rsem.at[slot],
            device_id={"gz": tile}, device_id_type=MESH,
        )

    def link_copy(section, slot):
        return pltpu.make_async_remote_copy(
            src_ref=link_out.at[section], dst_ref=link_in.at[slot],
            send_sem=link_ssem.at[section], recv_sem=link_rsem.at[slot],
            device_id={"gz": section}, device_id_type=MESH,
        )

    def first_pass(step, carry):
        block = first_block(step)
        for copy in loads(step):
            copy.wait()
        rows = pl.ds(pl.multiple_of(8 * block, 8), 8)
        edge_low = jnp.zeros((8, 128), jnp.float32)
        edge_high = jnp.zeros((8, 128), jnp.float32)
        alphas, betas = [], []
        for k in range(DEPTH):
            density = cons[0, k, rows, :]
            inverse = 1.0 / density
            velocity = [cons[1 + d, k, rows, :] * inverse for d in range(3)]
            kinetic = 0.5 * density * (
                velocity[0] * velocity[0] + velocity[1] * velocity[1] + velocity[2] * velocity[2]
            )
            pressure = (ADIABATIC - 1.0) * (cons[4, k, rows, :] - kinetic)
            sound = jnp.sqrt(ADIABATIC * pressure * inverse)
            radius = [jnp.abs(velocity[d]) + sound for d in range(3)]
            diagonal = METRIC[0] * radius[0] + METRIC[1] * radius[1] + METRIC[2] * radius[2]
            rdiag = 1.0 / diagonal
            half = (0.5 * METRIC[2]) * rdiag
            forward = (velocity[2] + radius[2]) * half
            backward = (radius[2] - velocity[2]) * half
            skew = (0.5 * METRIC[2] * COUPLING * ROOT2) * sound * rdiag
            for h in range(2):
                gain[2 * block + h, k] = tile_of(forward, h)
                gain[2 * block + h, 4 + k] = tile_of(backward, h)
                gain[2 * block + h, 8 + k] = tile_of(skew, h)
                scale[2 * block + h, k] = tile_of(rdiag, h)
            alphas.append((forward + skew, forward - skew, forward))
            betas.append((backward - skew, backward + skew, backward))

            r = [res[f, k, rows, :] for f in range(5)]
            total = r[0] + r[4]
            third = ROOT2 * r[3]
            source = [-(total + third), third - total, r[4] - r[0], -r[1], -r[2]]
            guess = [value * rdiag for value in source]
            pair = -total * rdiag
            cross = {}
            for d in range(2):
                weight = 0.5 * METRIC[d]
                plus = weight * (velocity[d] + radius[d])
                minus = weight * (velocity[d] - radius[d])
                mix = (weight * COUPLING) * sound
                outer = 2.0 * mix * guess[3 + d]
                inner = mix * pair
                extra = [outer, outer, None, None, None]
                extra[3 + d] = inner
                cross[d] = (
                    [plus * v if x is None else plus * v + x for v, x in zip(guess, extra)],
                    [minus * v if x is None else minus * v + x for v, x in zip(guess, extra)],
                )
            for e in range(5):
                n = 4 * e + k
                xp = pltpu.roll(cross[0][0][e], 1, 0)
                xm = pltpu.roll(cross[0][1][e], 7, 0)
                faces[0, block + 1, n : n + 1, :] = xp[0:1]
                faces[1, block, n : n + 1, :] = xm[7:8]
                yp, ym = cross[1][0][e], cross[1][1][e]
                base_part[n, rows, :] = (
                    source[e]
                    + jnp.where(sublane == 0, 0.0, xp)
                    + jnp.where(lane == 0, 0.0, pltpu.roll(yp, 1, 1))
                )
                up_part[n, rows, :] = (
                    jnp.where(sublane == 7, 0.0, xm)
                    + jnp.where(lane == 255, 0.0, pltpu.roll(ym, 255, 1))
                )
                edge_high = jnp.where(
                    small_lane == n, pltpu.roll(tile_of(yp, 1), (n + 1) % 128, 1), edge_high
                )
                edge_low = jnp.where(small_lane == n, pltpu.roll(tile_of(ym, 0), n, 1), edge_low)
        ys[0, rows, :] = edge_high
        ys[1, rows, :] = edge_low

        coefs = [None] * NCOEF
        for c in range(3):
            a = [alphas[k][c] for k in range(DEPTH)]
            b = [betas[k][c] for k in range(DEPTH)]
            lead = [None, a[0], a[0] * a[1], a[0] * a[1] * a[2]]
            trail = [None] * DEPTH
            trail[2] = b[3]
            trail[1] = b[3] * b[2]
            trail[0] = trail[1] * b[1]
            reply = [None] * DEPTH
            reply[3] = lead[3]
            reply[2] = lead[2] + b[3] * reply[3]
            reply[1] = lead[1] + b[2] * reply[2]
            reply[0] = 1.0 + b[1] * reply[1]
            coefs[c] = lead[3] * a[3]
            coefs[3 + c] = trail[0] * b[0]
            coefs[6 + c] = reply[0] * b[0]
            for h in range(2):
                for k in range(DEPTH):
                    pull[2 * block + h, 4 * c + k] = tile_of(reply[k], h)
                    if k < 3:
                        pull[2 * block + h, 12 + 3 * c + k] = tile_of(trail[k], h)
        for h in range(2):
            for j in range(NCOEF):
                coef_out[2 * block + h, j] = tile_of(coefs[j], h)

        return carry

    def first_send(step, carry):
        block = first_block(step)
        for h in range(2):
            tile = 2 * block + h

            @pl.when(tile != me)
            def _():
                coef_copy(tile, me).start()

        return carry

    lax.fori_loop(0, blocks, first_pass, 0)
    faces[gx, blocks * gx] = jnp.zeros((24, 256), jnp.float32)
    pl.semaphore_wait(barrier, sections + 2)
    face = pltpu.make_async_remote_copy(
        src_ref=faces.at[gx, blocks * (1 - gx)], dst_ref=faces.at[gx, blocks * gx],
        send_sem=halo_ssem.at[0], recv_sem=halo_rsem.at[0],
        device_id={"gx": 1 - gx}, device_id_type=MESH,
    )
    face.start()
    high = pltpu.make_async_remote_copy(
        src_ref=ys.at[0], dst_ref=yr.at[0], send_sem=halo_ssem.at[1], recv_sem=halo_rsem.at[1],
        device_id={"gy": above}, device_id_type=MESH,
    )
    high.start()
    low = pltpu.make_async_remote_copy(
        src_ref=ys.at[1], dst_ref=yr.at[1], send_sem=halo_ssem.at[2], recv_sem=halo_rsem.at[2],
        device_id={"gy": below}, device_id_type=MESH,
    )
    low.start()
    lax.fori_loop(0, blocks, first_send, 0)
    face.wait()
    high.wait()
    low.wait()

    def second_pass(step, carry):
        block = first_block(step)
        rows = pl.ds(pl.multiple_of(8 * block, 8), 8)
        left = jnp.where(gy > 0, yr[0, rows, :], 0.0)
        right = jnp.where(gy < gy_count - 1, yr[1, rows, :], 0.0)
        for e in range(5):
            base, side = [], []
            for k in range(DEPTH):
                n = 4 * e + k
                full = base_part[n, rows, :] + jnp.where(sublane == 0, faces[0, block, n : n + 1, :], 0.0)
                incoming = jnp.where(small_lane == 0, pltpu.roll(left, (128 - n) % 128, 1), 0.0)
                base.append((tile_of(full, 0) + incoming, tile_of(full, 1)))
                full = up_part[n, rows, :] + jnp.where(sublane == 7, faces[1, block + 1, n : n + 1, :], 0.0)
                incoming = jnp.where(small_lane == 127, pltpu.roll(right, 127 - n, 1), 0.0)
                side.append((tile_of(full, 0), tile_of(full, 1) + incoming))
            for h in range(2):
                tile = 2 * block + h
                f = [gain[tile, k] for k in range(DEPTH)]
                b = [gain[tile, 4 + k] for k in range(DEPTH)]
                if CLASS[e] != 2:
                    s = [gain[tile, 8 + k] for k in range(DEPTH)]
                    sign = 1.0 if CLASS[e] == 0 else -1.0
                    f = [x + sign * y for x, y in zip(f, s)]
                    b = [x - sign * y for x, y in zip(b, s)]
                lower = [base[0][h]]
                for k in range(1, DEPTH):
                    lower.append(base[k][h] + f[k - 1] * lower[k - 1])
                term_out[tile, e] = f[3] * lower[3]
                upper = lower[3] - side[3][h]
                part[tile, 4 * e + 3] = upper
                for k in (2, 1, 0):
                    upper = lower[k] - side[k][h] + b[k + 1] * upper
                    part[tile, 4 * e + k] = upper
                term_out[tile, 5 + e] = b[0] * upper
        for h in range(2):
            tile = 2 * block + h

            @pl.when(tile != me)
            def _():
                term_copy(tile, me).start()

        return carry

    lax.fori_loop(0, blocks, second_pass, 0)

    for j in range(NCOEF):
        coef_in[me, j] = coef_out[me, j]
    for j in range(NTERM):
        term_in[me, j] = term_out[me, j]

    def await_parts(step, carry):
        other = lax.rem(me + step, sections)
        coef_copy(other, other).wait_recv()
        term_copy(other, other).wait_recv()
        return carry

    lax.fori_loop(1, sections, await_parts, 0)

    zero = jnp.zeros((8, 128), jnp.float32)

    def go_up(section, carry):
        nxt = []
        for e in range(5):
            link_out[section, e] = carry[e]
            nxt.append(coef_in[section, CLASS[e]] * carry[e] + term_in[section, e])
        return tuple(nxt)

    lax.fori_loop(0, sections, go_up, (zero,) * 5)

    def go_down(step, carry):
        section = sections - 1 - step
        nxt = []
        for e in range(5):
            link_out[section, 5 + e] = carry[e]
            nxt.append(
                coef_in[section, 3 + CLASS[e]] * carry[e]
                + (term_in[section, 5 + e] + coef_in[section, 6 + CLASS[e]] * link_out[section, e])
            )
        return tuple(nxt)

    lax.fori_loop(0, sections, go_down, (zero,) * 5)

    def give_back(step, carry):
        link_copy(lax.rem(me + step, sections), me).start()
        return carry

    lax.fori_loop(1, sections, give_back, 0)
    for j in range(NTERM):
        link_in[me, j] = link_out[me, j]

    def store_copy(tile):
        rows = pl.ds(pl.multiple_of(8 * (tile // 2), 8), 8)
        columns = pl.ds(pl.multiple_of(128 * lax.rem(tile, 2), 128), 128)
        return pltpu.make_async_copy(
            result.at[tile], out_hbm.at[:, :, rows, columns], store_sem.at[tile]
        )

    def last_pass(step, carry):
        tile = lax.rem(me - step + sections, sections)

        @pl.when(step > 0)
        def _():
            link_copy(tile, tile).wait_recv()

        for k in range(DEPTH):
            value = []
            for e in range(5):
                c = CLASS[e]
                v = part[tile, 4 * e + k] + pull[tile, 4 * c + k] * link_in[tile, e]
                if k < 3:
                    v = v + pull[tile, 12 + 3 * c + k] * link_in[tile, 5 + e]
                else:
                    v = v + link_in[tile, 5 + e]
                value.append(v)
            rdiag = scale[tile, k]
            mean = 0.25 * (value[0] + value[1])
            halfway = 0.5 * value[2]
            result[tile, 0, k] = (mean + halfway) * rdiag
            result[tile, 1, k] = value[3] * rdiag
            result[tile, 2, k] = value[4] * rdiag
            result[tile, 3, k] = (0.5 / ROOT2) * (value[0] - value[1]) * rdiag
            result[tile, 4, k] = (mean - halfway) * rdiag
        store_copy(tile).start()
        return carry

    lax.fori_loop(0, sections, last_pass, 0)

    def finish(step, carry):
        other = lax.rem(me + step, sections)
        coef_copy(other, other).wait_send()
        term_copy(other, other).wait_send()
        link_copy(other, other).wait_send()
        return carry

    lax.fori_loop(1, sections, finish, 0)

    def drain(tile, carry):
        store_copy(tile).wait()
        return carry

    lax.fori_loop(0, sections, drain, 0)


def per_device(sections, gy_count, conserved, residual):
    rows, columns = conserved.shape[2], conserved.shape[3]
    blocks = rows // 8
    f32 = jnp.float32
    vmem = lambda *shape: pltpu.VMEM(shape, f32)
    dma = pltpu.SemaphoreType.DMA
    return pl.pallas_call(
        functools.partial(sweep_kernel, sections, gy_count, blocks),
        out_shape=jax.ShapeDtypeStruct(conserved.shape, f32),
        in_specs=[pl.BlockSpec(memory_space=pl.ANY)] * 2,
        out_specs=pl.BlockSpec(memory_space=pl.ANY),
        scratch_shapes=[
            vmem(*conserved.shape),
            vmem(*residual.shape),
            vmem(sections, 12, 8, 128),
            vmem(20, rows, columns),
            vmem(20, rows, columns),
            vmem(2, blocks + 1, 24, columns),
            vmem(sections, 21, 8, 128),
            vmem(sections, 20, 8, 128),
            vmem(sections, 4, 8, 128),
            vmem(sections, NCOEF, 8, 128),
            vmem(sections, NCOEF, 8, 128),
            vmem(sections, NTERM, 8, 128),
            vmem(sections, NTERM, 8, 128),
            vmem(sections, NTERM, 8, 128),
            vmem(sections, NTERM, 8, 128),
            vmem(2, rows, 128),
            vmem(2, rows, 128),
            vmem(sections, 5, 4, 8, 128),
            dma((2, blocks)),
            dma((sections,)),
            dma((sections,)),
            dma((sections,)),
            dma((sections,)),
            dma((sections,)),
            dma((sections,)),
            dma((3,)),
            dma((3,)),
            dma((sections,)),
        ],
        compiler_params=pltpu.CompilerParams(
            collective_id=0, has_side_effects=True, vmem_limit_bytes=48 << 20
        ),
    )(conserved, residual)


def solution(mesh):
    spec = P(None, "gz", "gx", "gy")
    return jax.shard_map(
        functools.partial(per_device, mesh.shape["gz"], mesh.shape["gy"]),
        mesh=mesh, in_specs=(spec, spec), out_specs=spec, check_vma=False,
    )
```

```python
import functools
import math

import jax
import jax.numpy as jnp
from jax import lax
from jax.experimental import pallas as pl
from jax.experimental.pallas import tpu as pltpu
from jax.sharding import PartitionSpec as P

MESH = pl.DeviceIdType.MESH
ROOT2 = math.sqrt(2.0)
ADIABATIC = 1.4
COUPLING = 0.7
METRIC = (0.1, 0.1, 1.0)
CLASS = (0, 1, 2, 2, 2)
DEPTH = 4
NCOEF = 9
NTERM = 10
GROUPS = ((2, 3, 4), (0, 1))
START = (0, 6)
SIZE = (6, 4)


def tile_of(value, half):
    return value[:, 128 * half : 128 * (half + 1)]


def sweep_kernel(
    sections, gy_count, blocks,
    cons_hbm, res_hbm, out,
    cons, res, gain, base_part, up_part, faces, pull, part, scale,
    coef_out, coef_in, term_out, term_in, link_out, link_in,
    ys, yr,
    load_sem, coef_ssem, coef_rsem, term_ssem, term_rsem, link_ssem, link_rsem,
    halo_ssem, halo_rsem,
):
    me = lax.axis_index("gz")
    gx = lax.axis_index("gx")
    gy = lax.axis_index("gy")
    above = lax.rem(gy + 1, gy_count)
    below = lax.rem(gy + gy_count - 1, gy_count)

    def first_block(step):
        return lax.rem(me // 2 + step, blocks)

    def loads(step):
        rows = pl.ds(pl.multiple_of(8 * first_block(step), 8), 8)
        return (
            pltpu.make_async_copy(cons_hbm.at[:, :, rows, :], cons.at[:, :, rows, :], load_sem.at[0, step]),
            pltpu.make_async_copy(res_hbm.at[:, :, rows, :], res.at[:, :, rows, :], load_sem.at[1, step]),
        )

    def start_load(step, carry):
        for copy in loads(step):
            copy.start()
        return carry

    lax.fori_loop(0, blocks, start_load, 0)

    barrier = pltpu.get_barrier_semaphore()

    def greet(step, carry):
        pl.semaphore_signal(
            barrier, inc=1, device_id={"gz": lax.rem(me + step, sections)}, device_id_type=MESH
        )
        return carry

    lax.fori_loop(1, sections, greet, 0)
    pl.semaphore_signal(barrier, inc=1, device_id={"gx": 1 - gx}, device_id_type=MESH)
    pl.semaphore_signal(barrier, inc=1, device_id={"gy": above}, device_id_type=MESH)
    pl.semaphore_signal(barrier, inc=1, device_id={"gy": below}, device_id_type=MESH)

    lane = lax.broadcasted_iota(jnp.int32, (8, 256), 1)
    sublane = lax.broadcasted_iota(jnp.int32, (8, 256), 0)
    small_lane = lax.broadcasted_iota(jnp.int32, (8, 128), 1)

    def coef_copy(tile, slot):
        return pltpu.make_async_remote_copy(
            src_ref=coef_out.at[tile], dst_ref=coef_in.at[slot],
            send_sem=coef_ssem.at[tile], recv_sem=coef_rsem.at[slot],
            device_id={"gz": tile}, device_id_type=MESH,
        )

    def term_copy(group, tile, slot):
        span = pl.ds(START[group], SIZE[group])
        return pltpu.make_async_remote_copy(
            src_ref=term_out.at[tile, span], dst_ref=term_in.at[slot, span],
            send_sem=term_ssem.at[group, tile], recv_sem=term_rsem.at[group, slot],
            device_id={"gz": tile}, device_id_type=MESH,
        )

    def link_copy(group, section, slot):
        span = pl.ds(START[group], SIZE[group])
        return pltpu.make_async_remote_copy(
            src_ref=link_out.at[section, span], dst_ref=link_in.at[slot, span],
            send_sem=link_ssem.at[group, section], recv_sem=link_rsem.at[group, slot],
            device_id={"gz": section}, device_id_type=MESH,
        )

    def first_pass(step, carry):
        block = first_block(step)
        for copy in loads(step):
            copy.wait()
        rows = pl.ds(pl.multiple_of(8 * block, 8), 8)
        edge_low = jnp.zeros((8, 128), jnp.float32)
        edge_high = jnp.zeros((8, 128), jnp.float32)
        alphas, betas = [], []
        for k in range(DEPTH):
            density = cons[0, k, rows, :]
            inverse = 1.0 / density
            velocity = [cons[1 + d, k, rows, :] * inverse for d in range(3)]
            kinetic = 0.5 * density * (
                velocity[0] * velocity[0] + velocity[1] * velocity[1] + velocity[2] * velocity[2]
            )
            pressure = (ADIABATIC - 1.0) * (cons[4, k, rows, :] - kinetic)
            sound = jnp.sqrt(ADIABATIC * pressure * inverse)
            radius = [jnp.abs(velocity[d]) + sound for d in range(3)]
            diagonal = METRIC[0] * radius[0] + METRIC[1] * radius[1] + METRIC[2] * radius[2]
            rdiag = 1.0 / diagonal
            half = (0.5 * METRIC[2]) * rdiag
            forward = (velocity[2] + radius[2]) * half
            backward = (radius[2] - velocity[2]) * half
            skew = (0.5 * METRIC[2] * COUPLING * ROOT2) * sound * rdiag
            for h in range(2):
                gain[2 * block + h, k] = tile_of(forward, h)
                gain[2 * block + h, 4 + k] = tile_of(backward, h)
                gain[2 * block + h, 8 + k] = tile_of(skew, h)
                scale[2 * block + h, k] = tile_of(rdiag, h)
            alphas.append((forward + skew, forward - skew, forward))
            betas.append((backward - skew, backward + skew, backward))

            r = [res[f, k, rows, :] for f in range(5)]
            total = r[0] + r[4]
            third = ROOT2 * r[3]
            source = [-(total + third), third - total, r[4] - r[0], -r[1], -r[2]]
            guess = [value * rdiag for value in source]
            pair = -total * rdiag
            cross = {}
            for d in range(2):
                weight = 0.5 * METRIC[d]
                plus = weight * (velocity[d] + radius[d])
                minus = weight * (velocity[d] - radius[d])
                mix = (weight * COUPLING) * sound
                outer = 2.0 * mix * guess[3 + d]
                inner = mix * pair
                extra = [outer, outer, None, None, None]
                extra[3 + d] = inner
                cross[d] = (
                    [plus * v if x is None else plus * v + x for v, x in zip(guess, extra)],
                    [minus * v if x is None else minus * v + x for v, x in zip(guess, extra)],
                )
            for e in range(5):
                n = 4 * e + k
                xp = pltpu.roll(cross[0][0][e], 1, 0)
                xm = pltpu.roll(cross[0][1][e], 7, 0)
                faces[0, block + 1, n : n + 1, :] = xp[0:1]
                faces[1, block, n : n + 1, :] = xm[7:8]
                yp, ym = cross[1][0][e], cross[1][1][e]
                base_part[n, rows, :] = (
                    source[e]
                    + jnp.where(sublane == 0, 0.0, xp)
                    + jnp.where(lane == 0, 0.0, pltpu.roll(yp, 1, 1))
                )
                up_part[n, rows, :] = (
                    jnp.where(sublane == 7, 0.0, xm)
                    + jnp.where(lane == 255, 0.0, pltpu.roll(ym, 255, 1))
                )
                edge_high = jnp.where(
                    small_lane == n, pltpu.roll(tile_of(yp, 1), (n + 1) % 128, 1), edge_high
                )
                edge_low = jnp.where(small_lane == n, pltpu.roll(tile_of(ym, 0), n, 1), edge_low)
        ys[0, rows, :] = edge_high
        ys[1, rows, :] = edge_low

        coefs = [None] * NCOEF
        for c in range(3):
            a = [alphas[k][c] for k in range(DEPTH)]
            b = [betas[k][c] for k in range(DEPTH)]
            lead = [None, a[0], a[0] * a[1], a[0] * a[1] * a[2]]
            trail = [None] * DEPTH
            trail[2] = b[3]
            trail[1] = b[3] * b[2]
            trail[0] = trail[1] * b[1]
            reply = [None] * DEPTH
            reply[3] = lead[3]
            reply[2] = lead[2] + b[3] * reply[3]
            reply[1] = lead[1] + b[2] * reply[2]
            reply[0] = 1.0 + b[1] * reply[1]
            coefs[c] = lead[3] * a[3]
            coefs[3 + c] = trail[0] * b[0]
            coefs[6 + c] = reply[0] * b[0]
            for h in range(2):
                for k in range(DEPTH):
                    pull[2 * block + h, 4 * c + k] = tile_of(reply[k], h)
                    if k < 3:
                        pull[2 * block + h, 12 + 3 * c + k] = tile_of(trail[k], h)
        for h in range(2):
            for j in range(NCOEF):
                coef_out[2 * block + h, j] = tile_of(coefs[j], h)

        return carry

    def first_send(step, carry):
        block = first_block(step)
        for h in range(2):
            tile = 2 * block + h

            @pl.when(tile != me)
            def _():
                coef_copy(tile, me).start()

        return carry

    lax.fori_loop(0, blocks, first_pass, 0)
    faces[gx, blocks * gx] = jnp.zeros((24, 256), jnp.float32)
    pl.semaphore_wait(barrier, sections + 2)
    face = pltpu.make_async_remote_copy(
        src_ref=faces.at[gx, blocks * (1 - gx)], dst_ref=faces.at[gx, blocks * gx],
        send_sem=halo_ssem.at[0], recv_sem=halo_rsem.at[0],
        device_id={"gx": 1 - gx}, device_id_type=MESH,
    )
    face.start()
    high = pltpu.make_async_remote_copy(
        src_ref=ys.at[0], dst_ref=yr.at[0], send_sem=halo_ssem.at[1], recv_sem=halo_rsem.at[1],
        device_id={"gy": above}, device_id_type=MESH,
    )
    high.start()
    low = pltpu.make_async_remote_copy(
        src_ref=ys.at[1], dst_ref=yr.at[1], send_sem=halo_ssem.at[2], recv_sem=halo_rsem.at[2],
        device_id={"gy": below}, device_id_type=MESH,
    )
    low.start()
    lax.fori_loop(0, blocks, first_send, 0)
    face.wait()
    high.wait()
    low.wait()

    def second_pass(group, step, carry):
        block = first_block(step)
        rows = pl.ds(pl.multiple_of(8 * block, 8), 8)
        left = jnp.where(gy > 0, yr[0, rows, :], 0.0)
        right = jnp.where(gy < gy_count - 1, yr[1, rows, :], 0.0)
        for place, e in enumerate(GROUPS[group]):
            base, side = [], []
            for k in range(DEPTH):
                n = 4 * e + k
                full = base_part[n, rows, :] + jnp.where(sublane == 0, faces[0, block, n : n + 1, :], 0.0)
                incoming = jnp.where(small_lane == 0, pltpu.roll(left, (128 - n) % 128, 1), 0.0)
                base.append((tile_of(full, 0) + incoming, tile_of(full, 1)))
                full = up_part[n, rows, :] + jnp.where(sublane == 7, faces[1, block + 1, n : n + 1, :], 0.0)
                incoming = jnp.where(small_lane == 127, pltpu.roll(right, 127 - n, 1), 0.0)
                side.append((tile_of(full, 0), tile_of(full, 1) + incoming))
            for h in range(2):
                tile = 2 * block + h
                f = [gain[tile, k] for k in range(DEPTH)]
                b = [gain[tile, 4 + k] for k in range(DEPTH)]
                if CLASS[e] != 2:
                    s = [gain[tile, 8 + k] for k in range(DEPTH)]
                    sign = 1.0 if CLASS[e] == 0 else -1.0
                    f = [x + sign * y for x, y in zip(f, s)]
                    b = [x - sign * y for x, y in zip(b, s)]
                lower = [base[0][h]]
                for k in range(1, DEPTH):
                    lower.append(base[k][h] + f[k - 1] * lower[k - 1])
                term_out[tile, START[group] + place] = f[3] * lower[3]
                upper = lower[3] - side[3][h]
                part[tile, 4 * e + 3] = upper
                for k in (2, 1, 0):
                    upper = lower[k] - side[k][h] + b[k + 1] * upper
                    part[tile, 4 * e + k] = upper
                term_out[tile, START[group] + SIZE[group] // 2 + place] = b[0] * upper
        for h in range(2):
            tile = 2 * block + h

            @pl.when(tile != me)
            def _():
                term_copy(group, tile, me).start()

        return carry

    for group in range(2):
        lax.fori_loop(0, blocks, functools.partial(second_pass, group), 0)

    for j in range(NCOEF):
        coef_in[me, j] = coef_out[me, j]
    for j in range(NTERM):
        term_in[me, j] = term_out[me, j]

    def await_coefs(step, carry):
        other = lax.rem(me + step, sections)
        coef_copy(other, other).wait_recv()
        return carry

    def await_terms(group, step, carry):
        other = lax.rem(me + step, sections)
        term_copy(group, other, other).wait_recv()
        return carry

    def go_up(group, section, carry):
        nxt = []
        for place, e in enumerate(GROUPS[group]):
            j = START[group] + place
            link_out[section, j] = carry[place]
            nxt.append(coef_in[section, CLASS[e]] * carry[place] + term_in[section, j])
        return tuple(nxt)

    def go_down(group, step, carry):
        section = sections - 1 - step
        nxt = []
        for place, e in enumerate(GROUPS[group]):
            low = START[group] + place
            high = low + SIZE[group] // 2
            link_out[section, high] = carry[place]
            nxt.append(
                coef_in[section, 3 + CLASS[e]] * carry[place]
                + (term_in[section, high] + coef_in[section, 6 + CLASS[e]] * link_out[section, low])
            )
        return tuple(nxt)

    def give_back(group, step, carry):
        link_copy(group, lax.rem(me + step, sections), me).start()
        return carry

    lax.fori_loop(1, sections, await_coefs, 0)
    zero = jnp.zeros((8, 128), jnp.float32)
    for group in range(2):
        count = len(GROUPS[group])
        lax.fori_loop(1, sections, functools.partial(await_terms, group), 0)
        lax.fori_loop(0, sections, functools.partial(go_up, group), (zero,) * count)
        lax.fori_loop(0, sections, functools.partial(go_down, group), (zero,) * count)
        lax.fori_loop(1, sections, functools.partial(give_back, group), 0)
    for j in range(NTERM):
        link_in[me, j] = link_out[me, j]

    def last_pass(step, carry):
        tile = lax.rem(me - step + sections, sections)
        rows = pl.ds(pl.multiple_of(8 * (tile // 2), 8), 8)
        columns = pl.ds(pl.multiple_of(128 * lax.rem(tile, 2), 128), 128)

        @pl.when(step > 0)
        def _():
            link_copy(0, tile, tile).wait_recv()
            link_copy(1, tile, tile).wait_recv()

        for k in range(DEPTH):
            value = []
            for e in range(5):
                c = CLASS[e]
                group = 0 if c == 2 else 1
                low = START[group] + GROUPS[group].index(e)
                high = low + SIZE[group] // 2
                v = part[tile, 4 * e + k] + pull[tile, 4 * c + k] * link_in[tile, low]
                if k < 3:
                    v = v + pull[tile, 12 + 3 * c + k] * link_in[tile, high]
                else:
                    v = v + link_in[tile, high]
                value.append(v)
            rdiag = scale[tile, k]
            mean = 0.25 * (value[0] + value[1])
            halfway = 0.5 * value[2]
            out[0, k, rows, columns] = (mean + halfway) * rdiag
            out[1, k, rows, columns] = value[3] * rdiag
            out[2, k, rows, columns] = value[4] * rdiag
            out[3, k, rows, columns] = (0.5 / ROOT2) * (value[0] - value[1]) * rdiag
            out[4, k, rows, columns] = (mean - halfway) * rdiag
        return carry

    lax.fori_loop(0, sections, last_pass, 0)

    def finish(step, carry):
        other = lax.rem(me + step, sections)
        coef_copy(other, other).wait_send()
        for group in range(2):
            term_copy(group, other, other).wait_send()
            link_copy(group, other, other).wait_send()
        return carry

    lax.fori_loop(1, sections, finish, 0)


def per_device(sections, gy_count, conserved, residual):
    rows, columns = conserved.shape[2], conserved.shape[3]
    blocks = rows // 8
    f32 = jnp.float32
    vmem = lambda *shape: pltpu.VMEM(shape, f32)
    dma = pltpu.SemaphoreType.DMA
    return pl.pallas_call(
        functools.partial(sweep_kernel, sections, gy_count, blocks),
        out_shape=pltpu.VMEM(conserved.shape, f32),
        in_specs=[pl.BlockSpec(memory_space=pltpu.HBM)] * 2,
        out_specs=pl.BlockSpec(memory_space=pltpu.VMEM),
        scratch_shapes=[
            vmem(*conserved.shape),
            vmem(*residual.shape),
            vmem(sections, 12, 8, 128),
            vmem(20, rows, columns),
            vmem(20, rows, columns),
            vmem(2, blocks + 1, 24, columns),
            vmem(sections, 21, 8, 128),
            vmem(sections, 20, 8, 128),
            vmem(sections, 4, 8, 128),
            vmem(sections, NCOEF, 8, 128),
            vmem(sections, NCOEF, 8, 128),
            vmem(sections, NTERM, 8, 128),
            vmem(sections, NTERM, 8, 128),
            vmem(sections, NTERM, 8, 128),
            vmem(sections, NTERM, 8, 128),
            vmem(2, rows, 128),
            vmem(2, rows, 128),
            dma((2, blocks)),
            dma((sections,)),
            dma((sections,)),
            dma((2, sections)),
            dma((2, sections)),
            dma((2, sections)),
            dma((2, sections)),
            dma((3,)),
            dma((3,)),
        ],
        compiler_params=pltpu.CompilerParams(
            collective_id=0, has_side_effects=True, vmem_limit_bytes=54 << 20
        ),
    )(conserved, residual)


def solution(mesh):
    spec = P(None, "gz", "gx", "gy")
    return jax.shard_map(
        functools.partial(per_device, mesh.shape["gz"], mesh.shape["gy"]),
        mesh=mesh, in_specs=(spec, spec), out_specs=spec, check_vma=False,
    )
```

```python
import functools
import math

import jax
import jax.numpy as jnp
from jax import lax
from jax.experimental import pallas as pl
from jax.experimental.pallas import tpu as pltpu
from jax.sharding import PartitionSpec as P

MESH = pl.DeviceIdType.MESH
ROOT2 = math.sqrt(2.0)
ADIABATIC = 1.4
COUPLING = 0.7
METRIC = (0.1, 0.1, 1.0)
CLASS = (0, 1, 2, 2, 2)
DEPTH = 4
NCOEF = 9
NTERM = 10
GROUPS = ((2, 3, 4), (0, 1))
START = (0, 6)
SIZE = (6, 4)


def tile_of(value, half):
    return value[:, 128 * half : 128 * (half + 1)]


def sweep_kernel(
    sections, gy_count, blocks,
    cons_hbm, res_hbm, out,
    cons, res, gain, base_part, up_part, faces, pull, part, scale,
    coef_out, coef_in, term_out, term_in, link_out, link_in,
    ys, yr,
    load_sem, coef_ssem, coef_rsem, term_ssem, term_rsem, link_ssem, link_rsem,
    halo_ssem, halo_rsem, plane_sem, near_sem,
):
    me = lax.axis_index("gz")
    gx = lax.axis_index("gx")
    gy = lax.axis_index("gy")
    above = lax.rem(gy + 1, gy_count)
    below = lax.rem(gy + gy_count - 1, gy_count)

    def first_block(step):
        return lax.rem(me // 2 + step, blocks)

    def loads(step):
        rows = pl.ds(pl.multiple_of(8 * first_block(step), 8), 8)
        return (
            pltpu.make_async_copy(cons_hbm.at[:, :, rows, :], cons.at[:, :, rows, :], load_sem.at[0, step]),
            pltpu.make_async_copy(res_hbm.at[:, :, rows, :], res.at[:, :, rows, :], load_sem.at[1, step]),
        )

    def start_load(step, carry):
        for copy in loads(step):
            copy.start()
        return carry

    barrier = pltpu.get_barrier_semaphore()

    def greet(step, carry):
        pl.semaphore_signal(
            barrier, inc=1, device_id={"gz": lax.rem(me + step, sections), "gx": 1}, device_id_type=MESH
        )
        return carry

    lax.fori_loop(0, blocks, start_load, 0)
    lax.fori_loop(1, sections, greet, 0)
    pl.semaphore_signal(barrier, inc=1, device_id={"gx": 0, "gy": above}, device_id_type=MESH)
    pl.semaphore_signal(barrier, inc=1, device_id={"gx": 0, "gy": below}, device_id_type=MESH)

    @pl.when(gx == 0)
    def _():
        pl.semaphore_signal(barrier, inc=1, device_id={"gx": 1}, device_id_type=MESH)

    def await_plane():
        @pl.when(gx == 1)
        def _():
            pl.semaphore_wait(barrier, 2 * sections - 1)
            pl.semaphore_signal(plane_sem, inc=1, device_id={"gx": 0}, device_id_type=MESH)

        @pl.when(gx == 0)
        def _():
            pl.semaphore_wait(plane_sem, 1)

    def await_neighbours():
        @pl.when(gx == 0)
        def _():
            pl.semaphore_wait(barrier, 4)
            pl.semaphore_signal(near_sem, inc=1, device_id={"gx": 1}, device_id_type=MESH)

        @pl.when(gx == 1)
        def _():
            pl.semaphore_wait(near_sem, 1)

    lane = lax.broadcasted_iota(jnp.int32, (8, 256), 1)
    sublane = lax.broadcasted_iota(jnp.int32, (8, 256), 0)
    small_lane = lax.broadcasted_iota(jnp.int32, (8, 128), 1)

    def coef_copy(tile, slot):
        return pltpu.make_async_remote_copy(
            src_ref=coef_out.at[tile], dst_ref=coef_in.at[slot], send_sem=coef_ssem, recv_sem=coef_rsem,
            device_id={"gz": tile}, device_id_type=MESH,
        )

    def term_copy(group, tile, slot):
        span = pl.ds(START[group], SIZE[group])
        return pltpu.make_async_remote_copy(
            src_ref=term_out.at[tile, span], dst_ref=term_in.at[slot, span],
            send_sem=term_ssem.at[group], recv_sem=term_rsem.at[group],
            device_id={"gz": tile}, device_id_type=MESH,
        )

    def link_copy(group, section, slot):
        span = pl.ds(START[group], SIZE[group])
        return pltpu.make_async_remote_copy(
            src_ref=link_out.at[section, span], dst_ref=link_in.at[slot, span],
            send_sem=link_ssem.at[group], recv_sem=link_rsem.at[group, slot],
            device_id={"gz": section}, device_id_type=MESH,
        )

    others = pl.ds(0, sections - 1)

    def coef_all():
        return pltpu.make_async_remote_copy(
            src_ref=coef_out.at[others], dst_ref=coef_in.at[others], send_sem=coef_ssem, recv_sem=coef_rsem,
            device_id={"gz": me}, device_id_type=MESH,
        )

    def term_all(group):
        span = pl.ds(START[group], SIZE[group])
        return pltpu.make_async_remote_copy(
            src_ref=term_out.at[others, span], dst_ref=term_in.at[others, span],
            send_sem=term_ssem.at[group], recv_sem=term_rsem.at[group],
            device_id={"gz": me}, device_id_type=MESH,
        )

    def link_sent(group):
        span = pl.ds(START[group], SIZE[group])
        return pltpu.make_async_remote_copy(
            src_ref=link_out.at[others, span], dst_ref=link_in.at[others, span],
            send_sem=link_ssem.at[group], recv_sem=link_rsem.at[group, 0],
            device_id={"gz": me}, device_id_type=MESH,
        )

    def first_pass(step, carry):
        block = first_block(step)
        for copy in loads(step):
            copy.wait()
        rows = pl.ds(pl.multiple_of(8 * block, 8), 8)
        edge_low = jnp.zeros((8, 128), jnp.float32)
        edge_high = jnp.zeros((8, 128), jnp.float32)
        alphas, betas = [], []
        for k in range(DEPTH):
            density = cons[0, k, rows, :]
            inverse = 1.0 / density
            velocity = [cons[1 + d, k, rows, :] * inverse for d in range(3)]
            kinetic = 0.5 * density * (
                velocity[0] * velocity[0] + velocity[1] * velocity[1] + velocity[2] * velocity[2]
            )
            pressure = (ADIABATIC - 1.0) * (cons[4, k, rows, :] - kinetic)
            sound = jnp.sqrt(ADIABATIC * pressure * inverse)
            radius = [jnp.abs(velocity[d]) + sound for d in range(3)]
            diagonal = METRIC[0] * radius[0] + METRIC[1] * radius[1] + METRIC[2] * radius[2]
            rdiag = 1.0 / diagonal
            half = (0.5 * METRIC[2]) * rdiag
            forward = (velocity[2] + radius[2]) * half
            backward = (radius[2] - velocity[2]) * half
            skew = (0.5 * METRIC[2] * COUPLING * ROOT2) * sound * rdiag
            for h in range(2):
                gain[2 * block + h, k] = tile_of(forward, h)
                gain[2 * block + h, 4 + k] = tile_of(backward, h)
                gain[2 * block + h, 8 + k] = tile_of(skew, h)
                scale[2 * block + h, k] = tile_of(rdiag, h)
            alphas.append((forward + skew, forward - skew, forward))
            betas.append((backward - skew, backward + skew, backward))

            r = [res[f, k, rows, :] for f in range(5)]
            total = r[0] + r[4]
            third = ROOT2 * r[3]
            source = [-(total + third), third - total, r[4] - r[0], -r[1], -r[2]]
            guess = [value * rdiag for value in source]
            pair = -total * rdiag
            cross = {}
            for d in range(2):
                weight = 0.5 * METRIC[d]
                plus = weight * (velocity[d] + radius[d])
                minus = weight * (velocity[d] - radius[d])
                mix = (weight * COUPLING) * sound
                outer = 2.0 * mix * guess[3 + d]
                inner = mix * pair
                extra = [outer, outer, None, None, None]
                extra[3 + d] = inner
                cross[d] = (
                    [plus * v if x is None else plus * v + x for v, x in zip(guess, extra)],
                    [minus * v if x is None else minus * v + x for v, x in zip(guess, extra)],
                )
            for e in range(5):
                n = 4 * e + k
                xp = pltpu.roll(cross[0][0][e], 1, 0)
                xm = pltpu.roll(cross[0][1][e], 7, 0)
                faces[0, block + 1, n : n + 1, :] = xp[0:1]
                faces[1, block, n : n + 1, :] = xm[7:8]
                yp, ym = cross[1][0][e], cross[1][1][e]
                base_part[n, rows, :] = (
                    source[e]
                    + jnp.where(sublane == 0, 0.0, xp)
                    + jnp.where(lane == 0, 0.0, pltpu.roll(yp, 1, 1))
                )
                up_part[n, rows, :] = (
                    jnp.where(sublane == 7, 0.0, xm)
                    + jnp.where(lane == 255, 0.0, pltpu.roll(ym, 255, 1))
                )
                edge_high = jnp.where(
                    small_lane == n, pltpu.roll(tile_of(yp, 1), (n + 1) % 128, 1), edge_high
                )
                edge_low = jnp.where(small_lane == n, pltpu.roll(tile_of(ym, 0), n, 1), edge_low)
        ys[0, rows, :] = edge_high
        ys[1, rows, :] = edge_low

        coefs = [None] * NCOEF
        for c in range(3):
            a = [alphas[k][c] for k in range(DEPTH)]
            b = [betas[k][c] for k in range(DEPTH)]
            lead = [None, a[0], a[0] * a[1], a[0] * a[1] * a[2]]
            trail = [None] * DEPTH
            trail[2] = b[3]
            trail[1] = b[3] * b[2]
            trail[0] = trail[1] * b[1]
            reply = [None] * DEPTH
            reply[3] = lead[3]
            reply[2] = lead[2] + b[3] * reply[3]
            reply[1] = lead[1] + b[2] * reply[2]
            reply[0] = 1.0 + b[1] * reply[1]
            coefs[c] = lead[3] * a[3]
            coefs[3 + c] = trail[0] * b[0]
            coefs[6 + c] = reply[0] * b[0]
            for h in range(2):
                for k in range(DEPTH):
                    pull[2 * block + h, 4 * c + k] = tile_of(reply[k], h)
                    if k < 3:
                        pull[2 * block + h, 12 + 3 * c + k] = tile_of(trail[k], h)
        for h in range(2):
            for j in range(NCOEF):
                coef_out[2 * block + h, j] = tile_of(coefs[j], h)

        pl.when(step == 0)(await_plane)
        for h in range(2):
            tile = 2 * block + h

            @pl.when(tile != me)
            def _():
                coef_copy(tile, me).start()

        return carry

    lax.fori_loop(0, blocks, first_pass, 0)
    faces[gx, blocks * gx] = jnp.zeros((24, 256), jnp.float32)
    await_neighbours()
    face = pltpu.make_async_remote_copy(
        src_ref=faces.at[gx, blocks * (1 - gx)], dst_ref=faces.at[gx, blocks * gx],
        send_sem=halo_ssem.at[0], recv_sem=halo_rsem.at[0],
        device_id={"gx": 1 - gx}, device_id_type=MESH,
    )
    face.start()
    high = pltpu.make_async_remote_copy(
        src_ref=ys.at[0], dst_ref=yr.at[0], send_sem=halo_ssem.at[1], recv_sem=halo_rsem.at[1],
        device_id={"gy": above}, device_id_type=MESH,
    )
    high.start()
    low = pltpu.make_async_remote_copy(
        src_ref=ys.at[1], dst_ref=yr.at[1], send_sem=halo_ssem.at[2], recv_sem=halo_rsem.at[2],
        device_id={"gy": below}, device_id_type=MESH,
    )
    low.start()
    face.wait()
    high.wait()
    low.wait()

    def second_pass(group, step, carry):
        block = first_block(step)
        rows = pl.ds(pl.multiple_of(8 * block, 8), 8)
        left = jnp.where(gy > 0, yr[0, rows, :], 0.0)
        right = jnp.where(gy < gy_count - 1, yr[1, rows, :], 0.0)
        for place, e in enumerate(GROUPS[group]):
            base, side = [], []
            for k in range(DEPTH):
                n = 4 * e + k
                full = base_part[n, rows, :] + jnp.where(sublane == 0, faces[0, block, n : n + 1, :], 0.0)
                incoming = jnp.where(small_lane == 0, pltpu.roll(left, (128 - n) % 128, 1), 0.0)
                base.append((tile_of(full, 0) + incoming, tile_of(full, 1)))
                full = up_part[n, rows, :] + jnp.where(sublane == 7, faces[1, block + 1, n : n + 1, :], 0.0)
                incoming = jnp.where(small_lane == 127, pltpu.roll(right, 127 - n, 1), 0.0)
                side.append((tile_of(full, 0), tile_of(full, 1) + incoming))
            for h in range(2):
                tile = 2 * block + h
                f = [gain[tile, k] for k in range(DEPTH)]
                b = [gain[tile, 4 + k] for k in range(DEPTH)]
                if CLASS[e] != 2:
                    s = [gain[tile, 8 + k] for k in range(DEPTH)]
                    sign = 1.0 if CLASS[e] == 0 else -1.0
                    f = [x + sign * y for x, y in zip(f, s)]
                    b = [x - sign * y for x, y in zip(b, s)]
                lower = [base[0][h]]
                for k in range(1, DEPTH):
                    lower.append(base[k][h] + f[k - 1] * lower[k - 1])
                term_out[tile, START[group] + place] = f[3] * lower[3]
                upper = lower[3] - side[3][h]
                part[tile, 4 * e + 3] = upper
                for k in (2, 1, 0):
                    upper = lower[k] - side[k][h] + b[k + 1] * upper
                    part[tile, 4 * e + k] = upper
                term_out[tile, START[group] + SIZE[group] // 2 + place] = b[0] * upper
        for h in range(2):
            tile = 2 * block + h

            @pl.when(tile != me)
            def _():
                term_copy(group, tile, me).start()

        return carry

    for group in range(2):
        lax.fori_loop(0, blocks, functools.partial(second_pass, group), 0)

    for j in range(NCOEF):
        coef_in[me, j] = coef_out[me, j]
    for j in range(NTERM):
        term_in[me, j] = term_out[me, j]

    def go_up(group, section, carry):
        nxt = []
        for place, e in enumerate(GROUPS[group]):
            j = START[group] + place
            link_out[section, j] = carry[place]
            nxt.append(coef_in[section, CLASS[e]] * carry[place] + term_in[section, j])
        return tuple(nxt)

    def go_down(group, step, carry):
        section = sections - 1 - step
        nxt = []
        for place, e in enumerate(GROUPS[group]):
            low = START[group] + place
            high = low + SIZE[group] // 2
            link_out[section, high] = carry[place]
            nxt.append(
                coef_in[section, 3 + CLASS[e]] * carry[place]
                + (term_in[section, high] + coef_in[section, 6 + CLASS[e]] * link_out[section, low])
            )
        return tuple(nxt)

    def give_back(group, step, carry):
        link_copy(group, lax.rem(me + step, sections), me).start()
        return carry

    coef_all().wait_recv()
    zero = jnp.zeros((8, 128), jnp.float32)
    for group in range(2):
        count = len(GROUPS[group])
        term_all(group).wait_recv()
        lax.fori_loop(0, sections, functools.partial(go_up, group), (zero,) * count, unroll=True)
        lax.fori_loop(0, sections, functools.partial(go_down, group), (zero,) * count, unroll=True)
        lax.fori_loop(1, sections, functools.partial(give_back, group), 0)
    for j in range(NTERM):
        link_in[me, j] = link_out[me, j]
    coef_all().wait_send()
    for group in range(2):
        term_all(group).wait_send()

    def last_pass(step, carry):
        tile = lax.rem(me - step + sections, sections)
        rows = pl.ds(pl.multiple_of(8 * (tile // 2), 8), 8)
        columns = pl.ds(pl.multiple_of(128 * lax.rem(tile, 2), 128), 128)

        @pl.when(step > 0)
        def _():
            link_copy(0, tile, tile).wait_recv()
            link_copy(1, tile, tile).wait_recv()

        for k in range(DEPTH):
            value = []
            for e in range(5):
                c = CLASS[e]
                group = 0 if c == 2 else 1
                low = START[group] + GROUPS[group].index(e)
                high = low + SIZE[group] // 2
                v = part[tile, 4 * e + k] + pull[tile, 4 * c + k] * link_in[tile, low]
                if k < 3:
                    v = v + pull[tile, 12 + 3 * c + k] * link_in[tile, high]
                else:
                    v = v + link_in[tile, high]
                value.append(v)
            rdiag = scale[tile, k]
            mean = 0.25 * (value[0] + value[1])
            halfway = 0.5 * value[2]
            out[0, k, rows, columns] = (mean + halfway) * rdiag
            out[1, k, rows, columns] = value[3] * rdiag
            out[2, k, rows, columns] = value[4] * rdiag
            out[3, k, rows, columns] = (0.5 / ROOT2) * (value[0] - value[1]) * rdiag
            out[4, k, rows, columns] = (mean - halfway) * rdiag
        return carry

    lax.fori_loop(0, sections, last_pass, 0)

    for group in range(2):
        link_sent(group).wait_send()


def per_device(sections, gy_count, conserved, residual):
    rows, columns = conserved.shape[2], conserved.shape[3]
    blocks = rows // 8
    f32 = jnp.float32
    vmem = lambda *shape: pltpu.VMEM(shape, f32)
    dma = pltpu.SemaphoreType.DMA
    return pl.pallas_call(
        functools.partial(sweep_kernel, sections, gy_count, blocks),
        out_shape=pltpu.VMEM(conserved.shape, f32),
        in_specs=[pl.BlockSpec(memory_space=pltpu.HBM)] * 2,
        out_specs=pl.BlockSpec(memory_space=pltpu.VMEM),
        scratch_shapes=[
            vmem(*conserved.shape),
            vmem(*residual.shape),
            vmem(sections, 12, 8, 128),
            vmem(20, rows, columns),
            vmem(20, rows, columns),
            vmem(2, blocks + 1, 24, columns),
            vmem(sections, 21, 8, 128),
            vmem(sections, 20, 8, 128),
            vmem(sections, 4, 8, 128),
            vmem(sections, NCOEF, 8, 128),
            vmem(sections, NCOEF, 8, 128),
            vmem(sections, NTERM, 8, 128),
            vmem(sections, NTERM, 8, 128),
            vmem(sections, NTERM, 8, 128),
            vmem(sections, NTERM, 8, 128),
            vmem(2, rows, 128),
            vmem(2, rows, 128),
            dma((2, blocks)),
            dma(()),
            dma(()),
            dma((2,)),
            dma((2,)),
            dma((2,)),
            dma((2, sections)),
            dma((3,)),
            dma((3,)),
            pltpu.SemaphoreType.REGULAR,
            pltpu.SemaphoreType.REGULAR,
        ],
        compiler_params=pltpu.CompilerParams(
            collective_id=0, has_side_effects=True, vmem_limit_bytes=54 << 20
        ),
    )(conserved, residual)


def solution(mesh):
    spec = P(None, "gz", "gx", "gy")
    return jax.shard_map(
        functools.partial(per_device, mesh.shape["gz"], mesh.shape["gy"]),
        mesh=mesh, in_specs=(spec, spec), out_specs=spec, check_vma=False,
    )
```

```python
import functools
import math

import jax
import jax.numpy as jnp
from jax import lax
from jax.experimental import pallas as pl
from jax.experimental.pallas import tpu as pltpu
from jax.sharding import PartitionSpec as P

MESH = pl.DeviceIdType.MESH
ROOT2 = math.sqrt(2.0)
ADIABATIC = 1.4
COUPLING = 0.7
METRIC = (0.1, 0.1, 1.0)
CLASS = (0, 1, 2, 2, 2)
DEPTH = 4
NCOEF = 9
NTERM = 10
GROUPS = ((2, 3, 4), (0, 1))
START = (0, 6)
SIZE = (6, 4)


def tile_of(value, half):
    return value[:, 128 * half : 128 * (half + 1)]


def sweep_kernel(
    sections, gy_count, blocks,
    cons_hbm, res_hbm, out,
    cons, res, gain, base_part, up_part, faces, pull, part, scale,
    coef_out, coef_in, term_out, term_in, link_out, link_in,
    ys, yr,
    load_sem, coef_ssem, coef_rsem, term_ssem, term_rsem, link_ssem, link_rsem,
    halo_ssem, halo_rsem, plane_sem, near_sem,
):
    me = lax.axis_index("gz")
    gx = lax.axis_index("gx")
    gy = lax.axis_index("gy")
    above = lax.rem(gy + 1, gy_count)
    below = lax.rem(gy + gy_count - 1, gy_count)

    def first_block(step):
        return lax.rem(me // 2 + step, blocks)

    def loads(step):
        rows = pl.ds(pl.multiple_of(8 * first_block(step), 8), 8)
        return (
            pltpu.make_async_copy(cons_hbm.at[:, :, rows, :], cons.at[:, :, rows, :], load_sem.at[0, step]),
            pltpu.make_async_copy(res_hbm.at[:, :, rows, :], res.at[:, :, rows, :], load_sem.at[1, step]),
        )

    def start_load(step, carry):
        for copy in loads(step):
            copy.start()
        return carry

    barrier = pltpu.get_barrier_semaphore()

    def greet(step, carry):
        pl.semaphore_signal(
            barrier, inc=1, device_id={"gz": lax.rem(me + step, sections), "gx": 1}, device_id_type=MESH
        )
        return carry

    lax.fori_loop(0, blocks, start_load, 0)
    lax.fori_loop(1, sections, greet, 0)
    pl.semaphore_signal(barrier, inc=1, device_id={"gx": 0, "gy": above}, device_id_type=MESH)
    pl.semaphore_signal(barrier, inc=1, device_id={"gx": 0, "gy": below}, device_id_type=MESH)

    @pl.when(gx == 0)
    def _():
        pl.semaphore_signal(barrier, inc=1, device_id={"gx": 1}, device_id_type=MESH)

    def await_plane():
        @pl.when(gx == 1)
        def _():
            pl.semaphore_wait(barrier, 2 * sections - 1)
            pl.semaphore_signal(plane_sem, inc=1, device_id={"gx": 0}, device_id_type=MESH)

        @pl.when(gx == 0)
        def _():
            pl.semaphore_wait(plane_sem, 1)

    def await_neighbours():
        @pl.when(gx == 0)
        def _():
            pl.semaphore_wait(barrier, 4)
            pl.semaphore_signal(near_sem, inc=1, device_id={"gx": 1}, device_id_type=MESH)

        @pl.when(gx == 1)
        def _():
            pl.semaphore_wait(near_sem, 1)

    lane = lax.broadcasted_iota(jnp.int32, (8, 256), 1)
    sublane = lax.broadcasted_iota(jnp.int32, (8, 256), 0)
    small_lane = lax.broadcasted_iota(jnp.int32, (8, 128), 1)

    def coef_copy(tile, slot):
        return pltpu.make_async_remote_copy(
            src_ref=coef_out.at[tile], dst_ref=coef_in.at[slot], send_sem=coef_ssem, recv_sem=coef_rsem,
            device_id={"gz": tile}, device_id_type=MESH,
        )

    def term_copy(group, tile, slot):
        span = pl.ds(START[group], SIZE[group])
        return pltpu.make_async_remote_copy(
            src_ref=term_out.at[tile, span], dst_ref=term_in.at[slot, span],
            send_sem=term_ssem.at[group], recv_sem=term_rsem.at[group],
            device_id={"gz": tile}, device_id_type=MESH,
        )

    def link_copy(group, section, slot):
        span = pl.ds(START[group], SIZE[group])
        return pltpu.make_async_remote_copy(
            src_ref=link_out.at[section, span], dst_ref=link_in.at[slot, span],
            send_sem=link_ssem.at[group], recv_sem=link_rsem.at[group, slot],
            device_id={"gz": section}, device_id_type=MESH,
        )

    others = pl.ds(0, sections - 1)

    def coef_all():
        return pltpu.make_async_remote_copy(
            src_ref=coef_out.at[others], dst_ref=coef_in.at[others], send_sem=coef_ssem, recv_sem=coef_rsem,
            device_id={"gz": me}, device_id_type=MESH,
        )

    def term_all(group):
        span = pl.ds(START[group], SIZE[group])
        return pltpu.make_async_remote_copy(
            src_ref=term_out.at[others, span], dst_ref=term_in.at[others, span],
            send_sem=term_ssem.at[group], recv_sem=term_rsem.at[group],
            device_id={"gz": me}, device_id_type=MESH,
        )

    def link_sent(group):
        span = pl.ds(START[group], SIZE[group])
        return pltpu.make_async_remote_copy(
            src_ref=link_out.at[others, span], dst_ref=link_in.at[others, span],
            send_sem=link_ssem.at[group], recv_sem=link_rsem.at[group, 0],
            device_id={"gz": me}, device_id_type=MESH,
        )

    def first_send(step, carry):
        for h in range(2):
            tile = 2 * first_block(step) + h

            @pl.when(tile != me)
            def _():
                coef_copy(tile, me).start()

        return carry

    def first_pass(step, carry):
        block = first_block(step)
        for copy in loads(step):
            copy.wait()
        rows = pl.ds(pl.multiple_of(8 * block, 8), 8)
        edge_low = jnp.zeros((8, 128), jnp.float32)
        edge_high = jnp.zeros((8, 128), jnp.float32)
        alphas, betas = [], []
        for k in range(DEPTH):
            density = cons[0, k, rows, :]
            inverse = 1.0 / density
            velocity = [cons[1 + d, k, rows, :] * inverse for d in range(3)]
            kinetic = 0.5 * density * (
                velocity[0] * velocity[0] + velocity[1] * velocity[1] + velocity[2] * velocity[2]
            )
            pressure = (ADIABATIC - 1.0) * (cons[4, k, rows, :] - kinetic)
            sound = jnp.sqrt(ADIABATIC * pressure * inverse)
            radius = [jnp.abs(velocity[d]) + sound for d in range(3)]
            diagonal = METRIC[0] * radius[0] + METRIC[1] * radius[1] + METRIC[2] * radius[2]
            rdiag = 1.0 / diagonal
            half = (0.5 * METRIC[2]) * rdiag
            forward = (velocity[2] + radius[2]) * half
            backward = (radius[2] - velocity[2]) * half
            skew = (0.5 * METRIC[2] * COUPLING * ROOT2) * sound * rdiag
            for h in range(2):
                gain[2 * block + h, k] = tile_of(forward, h)
                gain[2 * block + h, 4 + k] = tile_of(backward, h)
                gain[2 * block + h, 8 + k] = tile_of(skew, h)
                scale[2 * block + h, k] = tile_of(rdiag, h)
            alphas.append((forward + skew, forward - skew, forward))
            betas.append((backward - skew, backward + skew, backward))

            r = [res[f, k, rows, :] for f in range(5)]
            total = r[0] + r[4]
            third = ROOT2 * r[3]
            source = [-(total + third), third - total, r[4] - r[0], -r[1], -r[2]]
            guess = [value * rdiag for value in source]
            pair = -total * rdiag
            cross = {}
            for d in range(2):
                weight = 0.5 * METRIC[d]
                plus = weight * (velocity[d] + radius[d])
                minus = weight * (velocity[d] - radius[d])
                mix = (weight * COUPLING) * sound
                outer = 2.0 * mix * guess[3 + d]
                inner = mix * pair
                extra = [outer, outer, None, None, None]
                extra[3 + d] = inner
                cross[d] = (
                    [plus * v if x is None else plus * v + x for v, x in zip(guess, extra)],
                    [minus * v if x is None else minus * v + x for v, x in zip(guess, extra)],
                )
            for e in range(5):
                n = 4 * e + k
                xp = pltpu.roll(cross[0][0][e], 1, 0)
                xm = pltpu.roll(cross[0][1][e], 7, 0)
                faces[0, block + 1, n : n + 1, :] = xp[0:1]
                faces[1, block, n : n + 1, :] = xm[7:8]
                yp, ym = cross[1][0][e], cross[1][1][e]
                base_part[n, rows, :] = (
                    source[e]
                    + jnp.where(sublane == 0, 0.0, xp)
                    + jnp.where(lane == 0, 0.0, pltpu.roll(yp, 1, 1))
                )
                up_part[n, rows, :] = (
                    jnp.where(sublane == 7, 0.0, xm)
                    + jnp.where(lane == 255, 0.0, pltpu.roll(ym, 255, 1))
                )
                edge_high = jnp.where(
                    small_lane == n, pltpu.roll(tile_of(yp, 1), (n + 1) % 128, 1), edge_high
                )
                edge_low = jnp.where(small_lane == n, pltpu.roll(tile_of(ym, 0), n, 1), edge_low)
        ys[0, rows, :] = edge_high
        ys[1, rows, :] = edge_low

        coefs = [None] * NCOEF
        for c in range(3):
            a = [alphas[k][c] for k in range(DEPTH)]
            b = [betas[k][c] for k in range(DEPTH)]
            lead = [None, a[0], a[0] * a[1], a[0] * a[1] * a[2]]
            trail = [None] * DEPTH
            trail[2] = b[3]
            trail[1] = b[3] * b[2]
            trail[0] = trail[1] * b[1]
            reply = [None] * DEPTH
            reply[3] = lead[3]
            reply[2] = lead[2] + b[3] * reply[3]
            reply[1] = lead[1] + b[2] * reply[2]
            reply[0] = 1.0 + b[1] * reply[1]
            coefs[c] = lead[3] * a[3]
            coefs[3 + c] = trail[0] * b[0]
            coefs[6 + c] = reply[0] * b[0]
            for h in range(2):
                for k in range(DEPTH):
                    pull[2 * block + h, 4 * c + k] = tile_of(reply[k], h)
                    if k < 3:
                        pull[2 * block + h, 12 + 3 * c + k] = tile_of(trail[k], h)
        for h in range(2):
            for j in range(NCOEF):
                coef_out[2 * block + h, j] = tile_of(coefs[j], h)

        @pl.when(step == 4)
        def _():
            await_plane()
            lax.fori_loop(0, step, first_send, 0)

        @pl.when(step >= 4)
        def _():
            first_send(step, 0)

        return carry

    lax.fori_loop(0, blocks, first_pass, 0)
    faces[gx, blocks * gx] = jnp.zeros((24, 256), jnp.float32)
    await_neighbours()
    face = pltpu.make_async_remote_copy(
        src_ref=faces.at[gx, blocks * (1 - gx)], dst_ref=faces.at[gx, blocks * gx],
        send_sem=halo_ssem.at[0], recv_sem=halo_rsem.at[0],
        device_id={"gx": 1 - gx}, device_id_type=MESH,
    )
    face.start()
    high = pltpu.make_async_remote_copy(
        src_ref=ys.at[0], dst_ref=yr.at[0], send_sem=halo_ssem.at[1], recv_sem=halo_rsem.at[1],
        device_id={"gy": above}, device_id_type=MESH,
    )
    high.start()
    low = pltpu.make_async_remote_copy(
        src_ref=ys.at[1], dst_ref=yr.at[1], send_sem=halo_ssem.at[2], recv_sem=halo_rsem.at[2],
        device_id={"gy": below}, device_id_type=MESH,
    )
    low.start()
    face.wait()
    high.wait()
    low.wait()

    def second_pass(group, step, carry):
        block = first_block(step)
        rows = pl.ds(pl.multiple_of(8 * block, 8), 8)
        left = jnp.where(gy > 0, yr[0, rows, :], 0.0)
        right = jnp.where(gy < gy_count - 1, yr[1, rows, :], 0.0)
        for place, e in enumerate(GROUPS[group]):
            base, side = [], []
            for k in range(DEPTH):
                n = 4 * e + k
                full = base_part[n, rows, :] + jnp.where(sublane == 0, faces[0, block, n : n + 1, :], 0.0)
                incoming = jnp.where(small_lane == 0, pltpu.roll(left, (128 - n) % 128, 1), 0.0)
                base.append((tile_of(full, 0) + incoming, tile_of(full, 1)))
                full = up_part[n, rows, :] + jnp.where(sublane == 7, faces[1, block + 1, n : n + 1, :], 0.0)
                incoming = jnp.where(small_lane == 127, pltpu.roll(right, 127 - n, 1), 0.0)
                side.append((tile_of(full, 0), tile_of(full, 1) + incoming))
            for h in range(2):
                tile = 2 * block + h
                f = [gain[tile, k] for k in range(DEPTH)]
                b = [gain[tile, 4 + k] for k in range(DEPTH)]
                if CLASS[e] != 2:
                    s = [gain[tile, 8 + k] for k in range(DEPTH)]
                    sign = 1.0 if CLASS[e] == 0 else -1.0
                    f = [x + sign * y for x, y in zip(f, s)]
                    b = [x - sign * y for x, y in zip(b, s)]
                lower = [base[0][h]]
                for k in range(1, DEPTH):
                    lower.append(base[k][h] + f[k - 1] * lower[k - 1])
                term_out[tile, START[group] + place] = f[3] * lower[3]
                upper = lower[3] - side[3][h]
                part[tile, 4 * e + 3] = upper
                for k in (2, 1, 0):
                    upper = lower[k] - side[k][h] + b[k + 1] * upper
                    part[tile, 4 * e + k] = upper
                term_out[tile, START[group] + SIZE[group] // 2 + place] = b[0] * upper
        for h in range(2):
            tile = 2 * block + h

            @pl.when(tile != me)
            def _():
                term_copy(group, tile, me).start()

        return carry

    for group in range(2):
        lax.fori_loop(0, blocks, functools.partial(second_pass, group), 0)

    for j in range(NCOEF):
        coef_in[me, j] = coef_out[me, j]
    for j in range(NTERM):
        term_in[me, j] = term_out[me, j]

    def go_up(group, section, carry):
        nxt = []
        for place, e in enumerate(GROUPS[group]):
            j = START[group] + place
            link_out[section, j] = carry[place]
            nxt.append(coef_in[section, CLASS[e]] * carry[place] + term_in[section, j])
        return tuple(nxt)

    def go_down(group, step, carry):
        section = sections - 1 - step
        nxt = []
        for place, e in enumerate(GROUPS[group]):
            low = START[group] + place
            high = low + SIZE[group] // 2
            link_out[section, high] = carry[place]
            nxt.append(
                coef_in[section, 3 + CLASS[e]] * carry[place]
                + (term_in[section, high] + coef_in[section, 6 + CLASS[e]] * link_out[section, low])
            )
        return tuple(nxt)

    def give_back(group, step, carry):
        link_copy(group, lax.rem(me + step, sections), me).start()
        return carry

    coef_all().wait_recv()
    zero = jnp.zeros((8, 128), jnp.float32)
    for group in range(2):
        count = len(GROUPS[group])
        term_all(group).wait_recv()
        lax.fori_loop(0, sections, functools.partial(go_up, group), (zero,) * count, unroll=True)
        lax.fori_loop(0, sections, functools.partial(go_down, group), (zero,) * count, unroll=True)
        lax.fori_loop(1, sections, functools.partial(give_back, group), 0)
    for j in range(NTERM):
        link_in[me, j] = link_out[me, j]
    coef_all().wait_send()
    for group in range(2):
        term_all(group).wait_send()

    def last_pass(step, carry):
        tile = lax.rem(me - step + sections, sections)
        rows = pl.ds(pl.multiple_of(8 * (tile // 2), 8), 8)
        columns = pl.ds(pl.multiple_of(128 * lax.rem(tile, 2), 128), 128)

        @pl.when(step > 0)
        def _():
            link_copy(0, tile, tile).wait_recv()
            link_copy(1, tile, tile).wait_recv()

        for k in range(DEPTH):
            value = []
            for e in range(5):
                c = CLASS[e]
                group = 0 if c == 2 else 1
                low = START[group] + GROUPS[group].index(e)
                high = low + SIZE[group] // 2
                v = part[tile, 4 * e + k] + pull[tile, 4 * c + k] * link_in[tile, low]
                if k < 3:
                    v = v + pull[tile, 12 + 3 * c + k] * link_in[tile, high]
                else:
                    v = v + link_in[tile, high]
                value.append(v)
            rdiag = scale[tile, k]
            mean = 0.25 * (value[0] + value[1])
            halfway = 0.5 * value[2]
            out[0, k, rows, columns] = (mean + halfway) * rdiag
            out[1, k, rows, columns] = value[3] * rdiag
            out[2, k, rows, columns] = value[4] * rdiag
            out[3, k, rows, columns] = (0.5 / ROOT2) * (value[0] - value[1]) * rdiag
            out[4, k, rows, columns] = (mean - halfway) * rdiag
        return carry

    lax.fori_loop(0, sections, last_pass, 0)

    for group in range(2):
        link_sent(group).wait_send()


def per_device(sections, gy_count, conserved, residual):
    rows, columns = conserved.shape[2], conserved.shape[3]
    blocks = rows // 8
    f32 = jnp.float32
    vmem = lambda *shape: pltpu.VMEM(shape, f32)
    dma = pltpu.SemaphoreType.DMA
    return pl.pallas_call(
        functools.partial(sweep_kernel, sections, gy_count, blocks),
        out_shape=pltpu.VMEM(conserved.shape, f32),
        in_specs=[pl.BlockSpec(memory_space=pltpu.HBM)] * 2,
        out_specs=pl.BlockSpec(memory_space=pltpu.VMEM),
        scratch_shapes=[
            vmem(*conserved.shape),
            vmem(*residual.shape),
            vmem(sections, 12, 8, 128),
            vmem(20, rows, columns),
            vmem(20, rows, columns),
            vmem(2, blocks + 1, 24, columns),
            vmem(sections, 21, 8, 128),
            vmem(sections, 20, 8, 128),
            vmem(sections, 4, 8, 128),
            vmem(sections, NCOEF, 8, 128),
            vmem(sections, NCOEF, 8, 128),
            vmem(sections, NTERM, 8, 128),
            vmem(sections, NTERM, 8, 128),
            vmem(sections, NTERM, 8, 128),
            vmem(sections, NTERM, 8, 128),
            vmem(2, rows, 128),
            vmem(2, rows, 128),
            dma((2, blocks)),
            dma(()),
            dma(()),
            dma((2,)),
            dma((2,)),
            dma((2,)),
            dma((2, sections)),
            dma((3,)),
            dma((3,)),
            pltpu.SemaphoreType.REGULAR,
            pltpu.SemaphoreType.REGULAR,
        ],
        compiler_params=pltpu.CompilerParams(
            collective_id=0, has_side_effects=True, vmem_limit_bytes=54 << 20
        ),
    )(conserved, residual)


def solution(mesh):
    spec = P(None, "gz", "gx", "gy")
    return jax.shard_map(
        functools.partial(per_device, mesh.shape["gz"], mesh.shape["gy"]),
        mesh=mesh, in_specs=(spec, spec), out_specs=spec, check_vma=False,
    )
```

```python
import functools
import math

import jax
import jax.numpy as jnp
from jax import lax
from jax.experimental import pallas as pl
from jax.experimental.pallas import tpu as pltpu
from jax.sharding import PartitionSpec as P

MESH = pl.DeviceIdType.MESH
ROOT2 = math.sqrt(2.0)
ADIABATIC = 1.4
COUPLING = 0.7
METRIC = (0.1, 0.1, 1.0)
CLASS = (0, 1, 2, 2, 2)
DEPTH = 4
NCOEF = 9
NTERM = 10
GROUPS = ((2, 3, 4), (0, 1))
START = (0, 6)
SIZE = (6, 4)


def tile_of(value, half):
    return value[:, 128 * half : 128 * (half + 1)]


def sweep_kernel(
    sections, gy_count, blocks,
    cons_hbm, res_hbm, out,
    cons, res, gain, base_part, up_part, faces, pull, part, scale,
    coef_out, coef_in, term_out, term_in, link_out, link_in,
    ys, yr,
    load_sem, coef_ssem, coef_rsem, term_ssem, term_rsem, link_ssem, link_rsem,
    halo_ssem, halo_rsem, plane_sem, near_sem,
):
    me = lax.axis_index("gz")
    gx = lax.axis_index("gx")
    gy = lax.axis_index("gy")
    above = lax.rem(gy + 1, gy_count)
    below = lax.rem(gy + gy_count - 1, gy_count)

    def first_block(step):
        return lax.rem(me // 2 + step, blocks)

    def loads(step):
        rows = pl.ds(pl.multiple_of(8 * first_block(step), 8), 8)
        return (
            pltpu.make_async_copy(cons_hbm.at[:, :, rows, :], cons.at[:, :, rows, :], load_sem.at[0, step]),
            pltpu.make_async_copy(res_hbm.at[:, :, rows, :], res.at[:, :, rows, :], load_sem.at[1, step]),
        )

    def start_load(step, carry):
        for copy in loads(step):
            copy.start()
        return carry

    barrier = pltpu.get_barrier_semaphore()

    def greet(step, carry):
        pl.semaphore_signal(
            barrier, inc=1, device_id={"gz": lax.rem(me + step, sections), "gx": 1}, device_id_type=MESH
        )
        return carry

    lax.fori_loop(1, sections, greet, 0)
    pl.semaphore_signal(barrier, inc=1, device_id={"gx": 0, "gy": above}, device_id_type=MESH)
    pl.semaphore_signal(barrier, inc=1, device_id={"gx": 0, "gy": below}, device_id_type=MESH)

    @pl.when(gx == 0)
    def _():
        pl.semaphore_signal(barrier, inc=1, device_id={"gx": 1}, device_id_type=MESH)

    lax.fori_loop(0, blocks, start_load, 0)

    def await_plane():
        @pl.when(gx == 1)
        def _():
            pl.semaphore_wait(barrier, 2 * sections - 1)
            pl.semaphore_signal(plane_sem, inc=1, device_id={"gx": 0}, device_id_type=MESH)

        @pl.when(gx == 0)
        def _():
            pl.semaphore_wait(plane_sem, 1)

    def await_neighbours():
        @pl.when(gx == 0)
        def _():
            pl.semaphore_wait(barrier, 4)
            pl.semaphore_signal(near_sem, inc=1, device_id={"gx": 1}, device_id_type=MESH)

        @pl.when(gx == 1)
        def _():
            pl.semaphore_wait(near_sem, 1)

    lane = lax.broadcasted_iota(jnp.int32, (8, 256), 1)
    sublane = lax.broadcasted_iota(jnp.int32, (8, 256), 0)
    small_lane = lax.broadcasted_iota(jnp.int32, (8, 128), 1)

    def coef_copy(tile, slot):
        return pltpu.make_async_remote_copy(
            src_ref=coef_out.at[tile], dst_ref=coef_in.at[slot], send_sem=coef_ssem, recv_sem=coef_rsem,
            device_id={"gz": tile}, device_id_type=MESH,
        )

    def term_copy(group, tile, slot):
        span = pl.ds(START[group], SIZE[group])
        return pltpu.make_async_remote_copy(
            src_ref=term_out.at[tile, span], dst_ref=term_in.at[slot, span],
            send_sem=term_ssem.at[group], recv_sem=term_rsem.at[group],
            device_id={"gz": tile}, device_id_type=MESH,
        )

    def link_copy(group, section, slot):
        span = pl.ds(START[group], SIZE[group])
        return pltpu.make_async_remote_copy(
            src_ref=link_out.at[section, span], dst_ref=link_in.at[slot, span],
            send_sem=link_ssem.at[group], recv_sem=link_rsem.at[group, slot],
            device_id={"gz": section}, device_id_type=MESH,
        )

    others = pl.ds(0, sections - 1)

    def coef_all():
        return pltpu.make_async_remote_copy(
            src_ref=coef_out.at[others], dst_ref=coef_in.at[others], send_sem=coef_ssem, recv_sem=coef_rsem,
            device_id={"gz": me}, device_id_type=MESH,
        )

    def term_all(group):
        span = pl.ds(START[group], SIZE[group])
        return pltpu.make_async_remote_copy(
            src_ref=term_out.at[others, span], dst_ref=term_in.at[others, span],
            send_sem=term_ssem.at[group], recv_sem=term_rsem.at[group],
            device_id={"gz": me}, device_id_type=MESH,
        )

    def link_sent(group):
        span = pl.ds(START[group], SIZE[group])
        return pltpu.make_async_remote_copy(
            src_ref=link_out.at[others, span], dst_ref=link_in.at[others, span],
            send_sem=link_ssem.at[group], recv_sem=link_rsem.at[group, 0],
            device_id={"gz": me}, device_id_type=MESH,
        )

    def first_send(step, carry):
        for h in range(2):
            tile = 2 * first_block(step) + h

            @pl.when((tile != me) & ((step > 0) | (tile > me)))
            def _():
                coef_copy(tile, me).start()

        return carry

    def first_pass(step, carry):
        block = first_block(step)
        for copy in loads(step):
            copy.wait()
        rows = pl.ds(pl.multiple_of(8 * block, 8), 8)
        edge_low = jnp.zeros((8, 128), jnp.float32)
        edge_high = jnp.zeros((8, 128), jnp.float32)
        alphas, betas = [], []
        for k in range(DEPTH):
            density = cons[0, k, rows, :]
            inverse = 1.0 / density
            velocity = [cons[1 + d, k, rows, :] * inverse for d in range(3)]
            kinetic = 0.5 * density * (
                velocity[0] * velocity[0] + velocity[1] * velocity[1] + velocity[2] * velocity[2]
            )
            pressure = (ADIABATIC - 1.0) * (cons[4, k, rows, :] - kinetic)
            sound = jnp.sqrt(ADIABATIC * pressure * inverse)
            radius = [jnp.abs(velocity[d]) + sound for d in range(3)]
            diagonal = METRIC[0] * radius[0] + METRIC[1] * radius[1] + METRIC[2] * radius[2]
            rdiag = 1.0 / diagonal
            half = (0.5 * METRIC[2]) * rdiag
            forward = (velocity[2] + radius[2]) * half
            backward = (radius[2] - velocity[2]) * half
            skew = (0.5 * METRIC[2] * COUPLING * ROOT2) * sound * rdiag
            for h in range(2):
                gain[2 * block + h, k] = tile_of(forward, h)
                gain[2 * block + h, 4 + k] = tile_of(backward, h)
                gain[2 * block + h, 8 + k] = tile_of(skew, h)
                scale[2 * block + h, k] = tile_of(rdiag, h)
            alphas.append((forward + skew, forward - skew, forward))
            betas.append((backward - skew, backward + skew, backward))

            r = [res[f, k, rows, :] for f in range(5)]
            total = r[0] + r[4]
            third = ROOT2 * r[3]
            source = [-(total + third), third - total, r[4] - r[0], -r[1], -r[2]]
            guess = [value * rdiag for value in source]
            pair = -total * rdiag
            cross = {}
            for d in range(2):
                weight = 0.5 * METRIC[d]
                plus = weight * (velocity[d] + radius[d])
                minus = weight * (velocity[d] - radius[d])
                mix = (weight * COUPLING) * sound
                outer = 2.0 * mix * guess[3 + d]
                inner = mix * pair
                extra = [outer, outer, None, None, None]
                extra[3 + d] = inner
                cross[d] = (
                    [plus * v if x is None else plus * v + x for v, x in zip(guess, extra)],
                    [minus * v if x is None else minus * v + x for v, x in zip(guess, extra)],
                )
            for e in range(5):
                n = 4 * e + k
                xp = pltpu.roll(cross[0][0][e], 1, 0)
                xm = pltpu.roll(cross[0][1][e], 7, 0)
                faces[0, block + 1, n : n + 1, :] = xp[0:1]
                faces[1, block, n : n + 1, :] = xm[7:8]
                yp, ym = cross[1][0][e], cross[1][1][e]
                base_part[n, rows, :] = (
                    source[e]
                    + jnp.where(sublane == 0, 0.0, xp)
                    + jnp.where(lane == 0, 0.0, pltpu.roll(yp, 1, 1))
                )
                up_part[n, rows, :] = (
                    jnp.where(sublane == 7, 0.0, xm)
                    + jnp.where(lane == 255, 0.0, pltpu.roll(ym, 255, 1))
                )
                edge_high = jnp.where(
                    small_lane == n, pltpu.roll(tile_of(yp, 1), (n + 1) % 128, 1), edge_high
                )
                edge_low = jnp.where(small_lane == n, pltpu.roll(tile_of(ym, 0), n, 1), edge_low)
        ys[0, rows, :] = edge_high
        ys[1, rows, :] = edge_low

        coefs = [None] * NCOEF
        for c in range(3):
            a = [alphas[k][c] for k in range(DEPTH)]
            b = [betas[k][c] for k in range(DEPTH)]
            lead = [None, a[0], a[0] * a[1], a[0] * a[1] * a[2]]
            trail = [None] * DEPTH
            trail[2] = b[3]
            trail[1] = b[3] * b[2]
            trail[0] = trail[1] * b[1]
            reply = [None] * DEPTH
            reply[3] = lead[3]
            reply[2] = lead[2] + b[3] * reply[3]
            reply[1] = lead[1] + b[2] * reply[2]
            reply[0] = 1.0 + b[1] * reply[1]
            coefs[c] = lead[3] * a[3]
            coefs[3 + c] = trail[0] * b[0]
            coefs[6 + c] = reply[0] * b[0]
            for h in range(2):
                for k in range(DEPTH):
                    pull[2 * block + h, 4 * c + k] = tile_of(reply[k], h)
                    if k < 3:
                        pull[2 * block + h, 12 + 3 * c + k] = tile_of(trail[k], h)
        for h in range(2):
            for j in range(NCOEF):
                coef_out[2 * block + h, j] = tile_of(coefs[j], h)

        @pl.when(step == 5)
        def _():
            await_plane()
            lax.fori_loop(0, step, first_send, 0)

        @pl.when(step >= 5)
        def _():
            first_send(step, 0)

        return carry

    lax.fori_loop(0, blocks, first_pass, 0)

    odd = lax.rem(me, 2)

    @pl.when(odd == 1)
    def _():
        coef_copy(me - 1, me).start()

    faces[gx, blocks * gx] = jnp.zeros((24, 256), jnp.float32)
    await_neighbours()
    face = pltpu.make_async_remote_copy(
        src_ref=faces.at[gx, blocks * (1 - gx)], dst_ref=faces.at[gx, blocks * gx],
        send_sem=halo_ssem.at[0], recv_sem=halo_rsem.at[0],
        device_id={"gx": 1 - gx}, device_id_type=MESH,
    )
    face.start()
    high = pltpu.make_async_remote_copy(
        src_ref=ys.at[0], dst_ref=yr.at[0], send_sem=halo_ssem.at[1], recv_sem=halo_rsem.at[1],
        device_id={"gy": above}, device_id_type=MESH,
    )
    high.start()
    low = pltpu.make_async_remote_copy(
        src_ref=ys.at[1], dst_ref=yr.at[1], send_sem=halo_ssem.at[2], recv_sem=halo_rsem.at[2],
        device_id={"gy": below}, device_id_type=MESH,
    )
    low.start()
    face.wait()
    high.wait()
    low.wait()

    def second_pass(group, step, carry):
        block = first_block(step)
        rows = pl.ds(pl.multiple_of(8 * block, 8), 8)
        left = jnp.where(gy > 0, yr[0, rows, :], 0.0)
        right = jnp.where(gy < gy_count - 1, yr[1, rows, :], 0.0)
        for place, e in enumerate(GROUPS[group]):
            base, side = [], []
            for k in range(DEPTH):
                n = 4 * e + k
                full = base_part[n, rows, :] + jnp.where(sublane == 0, faces[0, block, n : n + 1, :], 0.0)
                incoming = jnp.where(small_lane == 0, pltpu.roll(left, (128 - n) % 128, 1), 0.0)
                base.append((tile_of(full, 0) + incoming, tile_of(full, 1)))
                full = up_part[n, rows, :] + jnp.where(sublane == 7, faces[1, block + 1, n : n + 1, :], 0.0)
                incoming = jnp.where(small_lane == 127, pltpu.roll(right, 127 - n, 1), 0.0)
                side.append((tile_of(full, 0), tile_of(full, 1) + incoming))
            for h in range(2):
                tile = 2 * block + h
                f = [gain[tile, k] for k in range(DEPTH)]
                b = [gain[tile, 4 + k] for k in range(DEPTH)]
                if CLASS[e] != 2:
                    s = [gain[tile, 8 + k] for k in range(DEPTH)]
                    sign = 1.0 if CLASS[e] == 0 else -1.0
                    f = [x + sign * y for x, y in zip(f, s)]
                    b = [x - sign * y for x, y in zip(b, s)]
                lower = [base[0][h]]
                for k in range(1, DEPTH):
                    lower.append(base[k][h] + f[k - 1] * lower[k - 1])
                term_out[tile, START[group] + place] = f[3] * lower[3]
                upper = lower[3] - side[3][h]
                part[tile, 4 * e + 3] = upper
                for k in (2, 1, 0):
                    upper = lower[k] - side[k][h] + b[k + 1] * upper
                    part[tile, 4 * e + k] = upper
                term_out[tile, START[group] + SIZE[group] // 2 + place] = b[0] * upper
        for h in range(2):
            tile = 2 * block + h

            @pl.when((tile != me) & ((step > 0) | (tile > me)))
            def _():
                term_copy(group, tile, me).start()

        return carry

    for group in range(2):
        lax.fori_loop(0, blocks, functools.partial(second_pass, group), 0)

        @pl.when(odd == 1)
        def _():
            term_copy(group, me - 1, me).start()


    for j in range(NCOEF):
        coef_in[me, j] = coef_out[me, j]
    for j in range(NTERM):
        term_in[me, j] = term_out[me, j]

    def go_up(group, section, carry):
        nxt = []
        for place, e in enumerate(GROUPS[group]):
            j = START[group] + place
            link_out[section, j] = carry[place]
            nxt.append(coef_in[section, CLASS[e]] * carry[place] + term_in[section, j])
        return tuple(nxt)

    def go_down(group, step, carry):
        section = sections - 1 - step
        nxt = []
        for place, e in enumerate(GROUPS[group]):
            low = START[group] + place
            high = low + SIZE[group] // 2
            link_out[section, high] = carry[place]
            nxt.append(
                coef_in[section, 3 + CLASS[e]] * carry[place]
                + (term_in[section, high] + coef_in[section, 6 + CLASS[e]] * link_out[section, low])
            )
        return tuple(nxt)

    def give_back(group, step, carry):
        link_copy(group, lax.rem(me + step, sections), me).start()
        return carry

    coef_all().wait_recv()
    zero = jnp.zeros((8, 128), jnp.float32)
    for group in range(2):
        count = len(GROUPS[group])
        term_all(group).wait_recv()
        lax.fori_loop(0, sections, functools.partial(go_up, group), (zero,) * count, unroll=True)
        lax.fori_loop(0, sections, functools.partial(go_down, group), (zero,) * count, unroll=True)
        lax.fori_loop(1, sections, functools.partial(give_back, group), 0)
    for j in range(NTERM):
        link_in[me, j] = link_out[me, j]
    coef_all().wait_send()
    for group in range(2):
        term_all(group).wait_send()

    def last_pass(step, carry):
        tile = lax.rem(me - step + sections, sections)
        rows = pl.ds(pl.multiple_of(8 * (tile // 2), 8), 8)
        columns = pl.ds(pl.multiple_of(128 * lax.rem(tile, 2), 128), 128)

        @pl.when(step > 0)
        def _():
            link_copy(0, tile, tile).wait_recv()
            link_copy(1, tile, tile).wait_recv()

        for k in range(DEPTH):
            value = []
            for e in range(5):
                c = CLASS[e]
                group = 0 if c == 2 else 1
                low = START[group] + GROUPS[group].index(e)
                high = low + SIZE[group] // 2
                v = part[tile, 4 * e + k] + pull[tile, 4 * c + k] * link_in[tile, low]
                if k < 3:
                    v = v + pull[tile, 12 + 3 * c + k] * link_in[tile, high]
                else:
                    v = v + link_in[tile, high]
                value.append(v)
            rdiag = scale[tile, k]
            mean = 0.25 * (value[0] + value[1])
            halfway = 0.5 * value[2]
            out[0, k, rows, columns] = (mean + halfway) * rdiag
            out[1, k, rows, columns] = value[3] * rdiag
            out[2, k, rows, columns] = value[4] * rdiag
            out[3, k, rows, columns] = (0.5 / ROOT2) * (value[0] - value[1]) * rdiag
            out[4, k, rows, columns] = (mean - halfway) * rdiag
        return carry

    lax.fori_loop(0, sections, last_pass, 0)

    for group in range(2):
        link_sent(group).wait_send()


def per_device(sections, gy_count, conserved, residual):
    rows, columns = conserved.shape[2], conserved.shape[3]
    blocks = rows // 8
    f32 = jnp.float32
    vmem = lambda *shape: pltpu.VMEM(shape, f32)
    dma = pltpu.SemaphoreType.DMA
    return pl.pallas_call(
        functools.partial(sweep_kernel, sections, gy_count, blocks),
        out_shape=pltpu.VMEM(conserved.shape, f32),
        in_specs=[pl.BlockSpec(memory_space=pltpu.HBM)] * 2,
        out_specs=pl.BlockSpec(memory_space=pltpu.VMEM),
        scratch_shapes=[
            vmem(*conserved.shape),
            vmem(*residual.shape),
            vmem(sections, 12, 8, 128),
            vmem(20, rows, columns),
            vmem(20, rows, columns),
            vmem(2, blocks + 1, 24, columns),
            vmem(sections, 21, 8, 128),
            vmem(sections, 20, 8, 128),
            vmem(sections, 4, 8, 128),
            vmem(sections, NCOEF, 8, 128),
            vmem(sections, NCOEF, 8, 128),
            vmem(sections, NTERM, 8, 128),
            vmem(sections, NTERM, 8, 128),
            vmem(sections, NTERM, 8, 128),
            vmem(sections, NTERM, 8, 128),
            vmem(2, rows, 128),
            vmem(2, rows, 128),
            dma((2, blocks)),
            dma(()),
            dma(()),
            dma((2,)),
            dma((2,)),
            dma((2,)),
            dma((2, sections)),
            dma((3,)),
            dma((3,)),
            pltpu.SemaphoreType.REGULAR,
            pltpu.SemaphoreType.REGULAR,
        ],
        compiler_params=pltpu.CompilerParams(
            collective_id=0, has_side_effects=True, vmem_limit_bytes=54 << 20
        ),
    )(conserved, residual)


def solution(mesh):
    spec = P(None, "gz", "gx", "gy")
    return jax.shard_map(
        functools.partial(per_device, mesh.shape["gz"], mesh.shape["gy"]),
        mesh=mesh, in_specs=(spec, spec), out_specs=spec, check_vma=False,
    )
```

```python
import functools
import math

import jax
import jax.numpy as jnp
from jax import lax
from jax.experimental import pallas as pl
from jax.experimental.pallas import tpu as pltpu
from jax.sharding import PartitionSpec as P

MESH = pl.DeviceIdType.MESH
ROOT2 = math.sqrt(2.0)
ADIABATIC = 1.4
COUPLING = 0.7
METRIC = (0.1, 0.1, 1.0)
CLASS = (0, 1, 2, 2, 2)
DEPTH = 4
NCOEF = 9
NTERM = 10
GROUPS = ((2, 3, 4), (0, 1))
START = (0, 6)
SIZE = (6, 4)


def tile_of(value, half):
    return value[:, 128 * half : 128 * (half + 1)]


def sweep_kernel(
    sections, gy_count, blocks,
    cons_hbm, res_hbm, out,
    cons, res, gain, base_part, up_part, faces, pull, part, scale,
    coef_out, coef_in, term_out, term_in, link_out, link_in,
    ys, yr,
    load_sem, coef_ssem, coef_rsem, term_ssem, term_rsem, link_ssem, link_rsem,
    halo_ssem, halo_rsem, plane_sem, near_sem,
):
    me = lax.axis_index("gz")
    gx = lax.axis_index("gx")
    gy = lax.axis_index("gy")
    above = lax.rem(gy + 1, gy_count)
    below = lax.rem(gy + gy_count - 1, gy_count)

    def first_block(step):
        return lax.rem(me // 2 + step, blocks)

    def loads(step):
        rows = pl.ds(pl.multiple_of(8 * first_block(step), 8), 8)
        return (
            pltpu.make_async_copy(cons_hbm.at[:, :, rows, :], cons.at[:, :, rows, :], load_sem.at[0, step]),
            pltpu.make_async_copy(res_hbm.at[:, :, rows, :], res.at[:, :, rows, :], load_sem.at[1, step]),
        )

    def start_load(step, carry):
        for copy in loads(step):
            copy.start()
        return carry

    barrier = pltpu.get_barrier_semaphore()

    def greet(step, carry):
        pl.semaphore_signal(
            barrier, inc=1, device_id={"gz": lax.rem(me + step, sections), "gx": 1}, device_id_type=MESH
        )
        return carry

    lax.fori_loop(1, sections, greet, 0)
    pl.semaphore_signal(barrier, inc=1, device_id={"gx": 0, "gy": above}, device_id_type=MESH)
    pl.semaphore_signal(barrier, inc=1, device_id={"gx": 0, "gy": below}, device_id_type=MESH)

    @pl.when(gx == 0)
    def _():
        pl.semaphore_signal(barrier, inc=1, device_id={"gx": 1}, device_id_type=MESH)

    lax.fori_loop(0, blocks, start_load, 0)

    def await_plane():
        @pl.when(gx == 1)
        def _():
            pl.semaphore_wait(barrier, 2 * sections - 1)
            pl.semaphore_signal(plane_sem, inc=1, device_id={"gx": 0}, device_id_type=MESH)

        @pl.when(gx == 0)
        def _():
            pl.semaphore_wait(plane_sem, 1)

    def await_neighbours():
        @pl.when(gx == 0)
        def _():
            pl.semaphore_wait(barrier, 4)
            pl.semaphore_signal(near_sem, inc=1, device_id={"gx": 1}, device_id_type=MESH)

        @pl.when(gx == 1)
        def _():
            pl.semaphore_wait(near_sem, 1)

    lane = lax.broadcasted_iota(jnp.int32, (8, 256), 1)
    sublane = lax.broadcasted_iota(jnp.int32, (8, 256), 0)
    small_lane = lax.broadcasted_iota(jnp.int32, (8, 128), 1)

    def coef_copy(tile, slot):
        return pltpu.make_async_remote_copy(
            src_ref=coef_out.at[tile], dst_ref=coef_in.at[slot], send_sem=coef_ssem, recv_sem=coef_rsem,
            device_id={"gz": tile}, device_id_type=MESH,
        )

    def term_copy(group, tile, slot):
        span = pl.ds(START[group], SIZE[group])
        return pltpu.make_async_remote_copy(
            src_ref=term_out.at[tile, span], dst_ref=term_in.at[slot, span],
            send_sem=term_ssem.at[group], recv_sem=term_rsem.at[group],
            device_id={"gz": tile}, device_id_type=MESH,
        )

    def link_copy(group, section, slot):
        span = pl.ds(START[group], SIZE[group])
        return pltpu.make_async_remote_copy(
            src_ref=link_out.at[section, span], dst_ref=link_in.at[slot, span],
            send_sem=link_ssem.at[group], recv_sem=link_rsem.at[group, slot],
            device_id={"gz": section}, device_id_type=MESH,
        )

    others = pl.ds(0, sections - 1)

    def coef_all():
        return pltpu.make_async_remote_copy(
            src_ref=coef_out.at[others], dst_ref=coef_in.at[others], send_sem=coef_ssem, recv_sem=coef_rsem,
            device_id={"gz": me}, device_id_type=MESH,
        )

    def term_all(group):
        span = pl.ds(START[group], SIZE[group])
        return pltpu.make_async_remote_copy(
            src_ref=term_out.at[others, span], dst_ref=term_in.at[others, span],
            send_sem=term_ssem.at[group], recv_sem=term_rsem.at[group],
            device_id={"gz": me}, device_id_type=MESH,
        )

    def link_sent(group):
        span = pl.ds(START[group], SIZE[group])
        return pltpu.make_async_remote_copy(
            src_ref=link_out.at[others, span], dst_ref=link_in.at[others, span],
            send_sem=link_ssem.at[group], recv_sem=link_rsem.at[group, 0],
            device_id={"gz": me}, device_id_type=MESH,
        )

    def first_send(step, carry):
        for h in range(2):
            tile = 2 * first_block(step) + h

            @pl.when((tile != me) & ((step > 0) | (tile > me)))
            def _():
                coef_copy(tile, me).start()

        return carry

    def first_pass(step, carry):
        block = first_block(step)
        for copy in loads(step):
            copy.wait()
        rows = pl.ds(pl.multiple_of(8 * block, 8), 8)
        edge_low = jnp.zeros((8, 128), jnp.float32)
        edge_high = jnp.zeros((8, 128), jnp.float32)
        alphas, betas = [], []
        for k in range(DEPTH):
            density = cons[0, k, rows, :]
            inverse = 1.0 / density
            velocity = [cons[1 + d, k, rows, :] * inverse for d in range(3)]
            kinetic = 0.5 * density * (
                velocity[0] * velocity[0] + velocity[1] * velocity[1] + velocity[2] * velocity[2]
            )
            pressure = (ADIABATIC - 1.0) * (cons[4, k, rows, :] - kinetic)
            sound = jnp.sqrt(ADIABATIC * pressure * inverse)
            radius = [jnp.abs(velocity[d]) + sound for d in range(3)]
            diagonal = METRIC[0] * radius[0] + METRIC[1] * radius[1] + METRIC[2] * radius[2]
            rdiag = 1.0 / diagonal
            half = (0.5 * METRIC[2]) * rdiag
            forward = (velocity[2] + radius[2]) * half
            backward = (radius[2] - velocity[2]) * half
            skew = (0.5 * METRIC[2] * COUPLING * ROOT2) * sound * rdiag
            for h in range(2):
                gain[2 * block + h, k] = tile_of(forward, h)
                gain[2 * block + h, 4 + k] = tile_of(backward, h)
                gain[2 * block + h, 8 + k] = tile_of(skew, h)
                scale[2 * block + h, k] = tile_of(rdiag, h)
            alphas.append((forward + skew, forward - skew, forward))
            betas.append((backward - skew, backward + skew, backward))

            r = [res[f, k, rows, :] for f in range(5)]
            total = r[0] + r[4]
            third = ROOT2 * r[3]
            source = [-(total + third), third - total, r[4] - r[0], -r[1], -r[2]]
            guess = [value * rdiag for value in source]
            pair = -total * rdiag
            cross = {}
            for d in range(2):
                weight = 0.5 * METRIC[d]
                plus = weight * (velocity[d] + radius[d])
                minus = weight * (velocity[d] - radius[d])
                mix = (weight * COUPLING) * sound
                outer = 2.0 * mix * guess[3 + d]
                inner = mix * pair
                extra = [outer, outer, None, None, None]
                extra[3 + d] = inner
                cross[d] = (
                    [plus * v if x is None else plus * v + x for v, x in zip(guess, extra)],
                    [minus * v if x is None else minus * v + x for v, x in zip(guess, extra)],
                )
            for e in range(5):
                n = 4 * e + k
                xp = pltpu.roll(cross[0][0][e], 1, 0)
                xm = pltpu.roll(cross[0][1][e], 7, 0)
                faces[0, block + 1, n : n + 1, :] = xp[0:1]
                faces[1, block, n : n + 1, :] = xm[7:8]
                yp, ym = cross[1][0][e], cross[1][1][e]
                base_part[n, rows, :] = (
                    source[e]
                    + jnp.where(sublane == 0, 0.0, xp)
                    + jnp.where(lane == 0, 0.0, pltpu.roll(yp, 1, 1))
                )
                up_part[n, rows, :] = (
                    jnp.where(sublane == 7, 0.0, xm)
                    + jnp.where(lane == 255, 0.0, pltpu.roll(ym, 255, 1))
                )
                edge_high = jnp.where(
                    small_lane == n, pltpu.roll(tile_of(yp, 1), (n + 1) % 128, 1), edge_high
                )
                edge_low = jnp.where(small_lane == n, pltpu.roll(tile_of(ym, 0), n, 1), edge_low)
        ys[0, rows, :] = edge_high
        ys[1, rows, :] = edge_low

        coefs = [None] * NCOEF
        for c in range(3):
            a = [alphas[k][c] for k in range(DEPTH)]
            b = [betas[k][c] for k in range(DEPTH)]
            lead = [None, a[0], a[0] * a[1], a[0] * a[1] * a[2]]
            trail = [None] * DEPTH
            trail[2] = b[3]
            trail[1] = b[3] * b[2]
            trail[0] = trail[1] * b[1]
            reply = [None] * DEPTH
            reply[3] = lead[3]
            reply[2] = lead[2] + b[3] * reply[3]
            reply[1] = lead[1] + b[2] * reply[2]
            reply[0] = 1.0 + b[1] * reply[1]
            coefs[c] = lead[3] * a[3]
            coefs[3 + c] = trail[0] * b[0]
            coefs[6 + c] = reply[0] * b[0]
            for h in range(2):
                for k in range(DEPTH):
                    pull[2 * block + h, 4 * c + k] = tile_of(reply[k], h)
                    if k < 3:
                        pull[2 * block + h, 12 + 3 * c + k] = tile_of(trail[k], h)
        for h in range(2):
            for j in range(NCOEF):
                coef_out[2 * block + h, j] = tile_of(coefs[j], h)

        @pl.when(step == 5)
        def _():
            await_plane()
            lax.fori_loop(0, step, first_send, 0)

        @pl.when(step >= 5)
        def _():
            first_send(step, 0)

        return carry

    lax.fori_loop(0, blocks, first_pass, 0)

    odd = lax.rem(me, 2)

    @pl.when(odd == 1)
    def _():
        coef_copy(me - 1, me).start()

    faces[gx, blocks * gx] = jnp.zeros((24, 256), jnp.float32)
    await_neighbours()
    face = pltpu.make_async_remote_copy(
        src_ref=faces.at[gx, blocks * (1 - gx)], dst_ref=faces.at[gx, blocks * gx],
        send_sem=halo_ssem.at[0], recv_sem=halo_rsem.at[0],
        device_id={"gx": 1 - gx}, device_id_type=MESH,
    )
    face.start()
    high = pltpu.make_async_remote_copy(
        src_ref=ys.at[0], dst_ref=yr.at[0], send_sem=halo_ssem.at[1], recv_sem=halo_rsem.at[1],
        device_id={"gy": above}, device_id_type=MESH,
    )
    high.start()
    low = pltpu.make_async_remote_copy(
        src_ref=ys.at[1], dst_ref=yr.at[1], send_sem=halo_ssem.at[2], recv_sem=halo_rsem.at[2],
        device_id={"gy": below}, device_id_type=MESH,
    )
    low.start()
    face.wait()
    high.wait()
    low.wait()

    def second_pass(group, step, carry):
        block = first_block(step)
        rows = pl.ds(pl.multiple_of(8 * block, 8), 8)
        left = jnp.where(gy > 0, yr[0, rows, :], 0.0)
        right = jnp.where(gy < gy_count - 1, yr[1, rows, :], 0.0)
        for place, e in enumerate(GROUPS[group]):
            base, side = [], []
            for k in range(DEPTH):
                n = 4 * e + k
                full = base_part[n, rows, :] + jnp.where(sublane == 0, faces[0, block, n : n + 1, :], 0.0)
                incoming = jnp.where(small_lane == 0, pltpu.roll(left, (128 - n) % 128, 1), 0.0)
                base.append((tile_of(full, 0) + incoming, tile_of(full, 1)))
                full = up_part[n, rows, :] + jnp.where(sublane == 7, faces[1, block + 1, n : n + 1, :], 0.0)
                incoming = jnp.where(small_lane == 127, pltpu.roll(right, 127 - n, 1), 0.0)
                side.append((tile_of(full, 0), tile_of(full, 1) + incoming))
            for h in range(2):
                tile = 2 * block + h
                f = [gain[tile, k] for k in range(DEPTH)]
                b = [gain[tile, 4 + k] for k in range(DEPTH)]
                if CLASS[e] != 2:
                    s = [gain[tile, 8 + k] for k in range(DEPTH)]
                    sign = 1.0 if CLASS[e] == 0 else -1.0
                    f = [x + sign * y for x, y in zip(f, s)]
                    b = [x - sign * y for x, y in zip(b, s)]
                lower = [base[0][h]]
                for k in range(1, DEPTH):
                    lower.append(base[k][h] + f[k - 1] * lower[k - 1])
                term_out[tile, START[group] + place] = f[3] * lower[3]
                upper = lower[3] - side[3][h]
                part[tile, 4 * e + 3] = upper
                for k in (2, 1, 0):
                    upper = lower[k] - side[k][h] + b[k + 1] * upper
                    part[tile, 4 * e + k] = upper
                term_out[tile, START[group] + SIZE[group] // 2 + place] = b[0] * upper
        for h in range(2):
            tile = 2 * block + h

            @pl.when((tile != me) & ((step > 0) | (tile > me)))
            def _():
                term_copy(group, tile, me).start()

        return carry

    for group in range(2):
        lax.fori_loop(0, blocks, functools.partial(second_pass, group), 0)

        @pl.when(odd == 1)
        def _():
            term_copy(group, me - 1, me).start()


    for j in range(NCOEF):
        coef_in[me, j] = coef_out[me, j]
    for j in range(NTERM):
        term_in[me, j] = term_out[me, j]

    def go_up(group, section, carry):
        nxt = []
        for place, e in enumerate(GROUPS[group]):
            j = START[group] + place
            link_out[section, j] = carry[place]
            nxt.append(coef_in[section, CLASS[e]] * carry[place] + term_in[section, j])
        return tuple(nxt)

    def go_down(group, step, carry):
        section = sections - 1 - step
        nxt = []
        for place, e in enumerate(GROUPS[group]):
            low = START[group] + place
            high = low + SIZE[group] // 2
            link_out[section, high] = carry[place]
            nxt.append(
                coef_in[section, 3 + CLASS[e]] * carry[place]
                + (term_in[section, high] + coef_in[section, 6 + CLASS[e]] * link_out[section, low])
            )
        return tuple(nxt)

    def give_back(group, step, carry):
        link_copy(group, lax.rem(me + step, sections), me).start()
        return carry

    coef_all().wait_recv()
    zero = jnp.zeros((8, 128), jnp.float32)
    for group in range(2):
        count = len(GROUPS[group])
        term_all(group).wait_recv()
        lax.fori_loop(0, sections, functools.partial(go_up, group), (zero,) * count, unroll=True)
        lax.fori_loop(0, sections, functools.partial(go_down, group), (zero,) * count, unroll=True)
        lax.fori_loop(1, sections, functools.partial(give_back, group), 0)
    for j in range(NTERM):
        link_in[me, j] = link_out[me, j]
    coef_all().wait_send()
    for group in range(2):
        term_all(group).wait_send()

    def solved(tile, k, e):
        c = CLASS[e]
        group = 0 if c == 2 else 1
        low = START[group] + GROUPS[group].index(e)
        high = low + SIZE[group] // 2
        v = part[tile, 4 * e + k] + pull[tile, 4 * c + k] * link_in[tile, low]
        if k < 3:
            return v + pull[tile, 12 + 3 * c + k] * link_in[tile, high]
        return v + link_in[tile, high]

    def last_pass(group, step, carry):
        tile = lax.rem(me - step + sections, sections)
        rows = pl.ds(pl.multiple_of(8 * (tile // 2), 8), 8)
        columns = pl.ds(pl.multiple_of(128 * lax.rem(tile, 2), 128), 128)

        @pl.when(step > 0)
        def _():
            link_copy(group, tile, tile).wait_recv()

        for k in range(DEPTH):
            rdiag = scale[tile, k]
            if group == 0:
                halfway = 0.5 * solved(tile, k, 2)
                out[0, k, rows, columns] = halfway * rdiag
                out[1, k, rows, columns] = solved(tile, k, 3) * rdiag
                out[2, k, rows, columns] = solved(tile, k, 4) * rdiag
            else:
                p, q = solved(tile, k, 0), solved(tile, k, 1)
                mean = 0.25 * (p + q) * rdiag
                halfway = out[0, k, rows, columns]
                out[0, k, rows, columns] = mean + halfway
                out[3, k, rows, columns] = (0.5 / ROOT2) * (p - q) * rdiag
                out[4, k, rows, columns] = mean - halfway
        return carry

    for group in range(2):
        lax.fori_loop(0, sections, functools.partial(last_pass, group), 0)

    for group in range(2):
        link_sent(group).wait_send()


def per_device(sections, gy_count, conserved, residual):
    rows, columns = conserved.shape[2], conserved.shape[3]
    blocks = rows // 8
    f32 = jnp.float32
    vmem = lambda *shape: pltpu.VMEM(shape, f32)
    dma = pltpu.SemaphoreType.DMA
    return pl.pallas_call(
        functools.partial(sweep_kernel, sections, gy_count, blocks),
        out_shape=pltpu.VMEM(conserved.shape, f32),
        in_specs=[pl.BlockSpec(memory_space=pltpu.HBM)] * 2,
        out_specs=pl.BlockSpec(memory_space=pltpu.VMEM),
        scratch_shapes=[
            vmem(*conserved.shape),
            vmem(*residual.shape),
            vmem(sections, 12, 8, 128),
            vmem(20, rows, columns),
            vmem(20, rows, columns),
            vmem(2, blocks + 1, 24, columns),
            vmem(sections, 21, 8, 128),
            vmem(sections, 20, 8, 128),
            vmem(sections, 4, 8, 128),
            vmem(sections, NCOEF, 8, 128),
            vmem(sections, NCOEF, 8, 128),
            vmem(sections, NTERM, 8, 128),
            vmem(sections, NTERM, 8, 128),
            vmem(sections, NTERM, 8, 128),
            vmem(sections, NTERM, 8, 128),
            vmem(2, rows, 128),
            vmem(2, rows, 128),
            dma((2, blocks)),
            dma(()),
            dma(()),
            dma((2,)),
            dma((2,)),
            dma((2,)),
            dma((2, sections)),
            dma((3,)),
            dma((3,)),
            pltpu.SemaphoreType.REGULAR,
            pltpu.SemaphoreType.REGULAR,
        ],
        compiler_params=pltpu.CompilerParams(
            collective_id=0, has_side_effects=True, vmem_limit_bytes=54 << 20
        ),
    )(conserved, residual)


def solution(mesh):
    spec = P(None, "gz", "gx", "gy")
    return jax.shard_map(
        functools.partial(per_device, mesh.shape["gz"], mesh.shape["gy"]),
        mesh=mesh, in_specs=(spec, spec), out_specs=spec, check_vma=False,
    )
```

```python
import functools
import math

import jax
import jax.numpy as jnp
from jax import lax
from jax.experimental import pallas as pl
from jax.experimental.pallas import tpu as pltpu
from jax.sharding import PartitionSpec as P

MESH = pl.DeviceIdType.MESH
ROOT2 = math.sqrt(2.0)
ADIABATIC = 1.4
COUPLING = 0.7
METRIC = (0.1, 0.1, 1.0)
CLASS = (0, 1, 2, 2, 2)
DEPTH = 4
NCOEF = 9
NTERM = 10
GROUPS = ((2, 3, 4), (0, 1))
START = (0, 6)
SIZE = (6, 4)


def tile_of(value, half):
    return value[:, 128 * half : 128 * (half + 1)]


def sweep_kernel(
    sections, gy_count, blocks,
    cons_hbm, res_hbm, out,
    cons, res, gain, base_part, up_part, faces, pull, part, scale,
    coef_out, coef_in, term_out, term_in, link_out, link_in,
    ys, yr,
    load_sem, coef_ssem, coef_rsem, term_ssem, term_rsem, link_ssem, link_rsem,
    halo_ssem, halo_rsem, plane_sem, near_sem,
):
    me = lax.axis_index("gz")
    gx = lax.axis_index("gx")
    gy = lax.axis_index("gy")
    above = lax.rem(gy + 1, gy_count)
    below = lax.rem(gy + gy_count - 1, gy_count)

    def first_block(step):
        return lax.rem(me // 2 + step, blocks)

    def loads(step):
        rows = pl.ds(pl.multiple_of(8 * first_block(step), 8), 8)
        return (
            pltpu.make_async_copy(cons_hbm.at[:, :, rows, :], cons.at[:, :, rows, :], load_sem.at[0, step]),
            pltpu.make_async_copy(res_hbm.at[:, :, rows, :], res.at[:, :, rows, :], load_sem.at[1, step]),
        )

    def start_load(step, carry):
        for copy in loads(step):
            copy.start()
        return carry

    barrier = pltpu.get_barrier_semaphore()

    def greet(step, carry):
        pl.semaphore_signal(
            barrier, inc=1, device_id={"gz": lax.rem(me + step, sections), "gx": 1}, device_id_type=MESH
        )
        return carry

    lax.fori_loop(1, sections, greet, 0)
    pl.semaphore_signal(barrier, inc=1, device_id={"gx": 0, "gy": above}, device_id_type=MESH)
    pl.semaphore_signal(barrier, inc=1, device_id={"gx": 0, "gy": below}, device_id_type=MESH)

    @pl.when(gx == 0)
    def _():
        pl.semaphore_signal(barrier, inc=1, device_id={"gx": 1}, device_id_type=MESH)

    lax.fori_loop(0, blocks, start_load, 0)

    def await_plane():
        @pl.when(gx == 1)
        def _():
            pl.semaphore_wait(barrier, 2 * sections - 1)
            pl.semaphore_signal(plane_sem, inc=1, device_id={"gx": 0}, device_id_type=MESH)

        @pl.when(gx == 0)
        def _():
            pl.semaphore_wait(plane_sem, 1)

    def await_neighbours():
        @pl.when(gx == 0)
        def _():
            pl.semaphore_wait(barrier, 4)
            pl.semaphore_signal(near_sem, inc=1, device_id={"gx": 1}, device_id_type=MESH)

        @pl.when(gx == 1)
        def _():
            pl.semaphore_wait(near_sem, 1)

    lane = lax.broadcasted_iota(jnp.int32, (8, 256), 1)
    sublane = lax.broadcasted_iota(jnp.int32, (8, 256), 0)
    small_lane = lax.broadcasted_iota(jnp.int32, (8, 128), 1)

    def coef_copy(tile, slot):
        return pltpu.make_async_remote_copy(
            src_ref=coef_out.at[tile], dst_ref=coef_in.at[slot], send_sem=coef_ssem, recv_sem=coef_rsem,
            device_id={"gz": tile}, device_id_type=MESH,
        )

    def term_copy(group, tile, slot):
        span = pl.ds(START[group], SIZE[group])
        return pltpu.make_async_remote_copy(
            src_ref=term_out.at[tile, span], dst_ref=term_in.at[slot, span],
            send_sem=term_ssem.at[group], recv_sem=term_rsem.at[group],
            device_id={"gz": tile}, device_id_type=MESH,
        )

    def link_copy(group, section, slot):
        span = pl.ds(START[group], SIZE[group])
        return pltpu.make_async_remote_copy(
            src_ref=link_out.at[section, span], dst_ref=link_in.at[slot, span],
            send_sem=link_ssem.at[group], recv_sem=link_rsem.at[group, slot],
            device_id={"gz": section}, device_id_type=MESH,
        )

    others = pl.ds(0, sections - 1)

    def coef_all():
        return pltpu.make_async_remote_copy(
            src_ref=coef_out.at[others], dst_ref=coef_in.at[others], send_sem=coef_ssem, recv_sem=coef_rsem,
            device_id={"gz": me}, device_id_type=MESH,
        )

    def term_all(group):
        span = pl.ds(START[group], SIZE[group])
        return pltpu.make_async_remote_copy(
            src_ref=term_out.at[others, span], dst_ref=term_in.at[others, span],
            send_sem=term_ssem.at[group], recv_sem=term_rsem.at[group],
            device_id={"gz": me}, device_id_type=MESH,
        )

    def link_sent(group):
        span = pl.ds(START[group], SIZE[group])
        return pltpu.make_async_remote_copy(
            src_ref=link_out.at[others, span], dst_ref=link_in.at[others, span],
            send_sem=link_ssem.at[group], recv_sem=link_rsem.at[group, 0],
            device_id={"gz": me}, device_id_type=MESH,
        )

    def first_send(step, carry):
        for h in range(2):
            tile = 2 * first_block(step) + h

            @pl.when((tile != me) & ((step > 0) | (tile > me)))
            def _():
                coef_copy(tile, me).start()

        return carry

    def first_pass(step, carry):
        block = first_block(step)
        for copy in loads(step):
            copy.wait()
        rows = pl.ds(pl.multiple_of(8 * block, 8), 8)
        edge_low = jnp.zeros((8, 128), jnp.float32)
        edge_high = jnp.zeros((8, 128), jnp.float32)
        alphas, betas = [], []
        for k in range(DEPTH):
            density = cons[0, k, rows, :]
            inverse = 1.0 / density
            velocity = [cons[1 + d, k, rows, :] * inverse for d in range(3)]
            kinetic = 0.5 * density * (
                velocity[0] * velocity[0] + velocity[1] * velocity[1] + velocity[2] * velocity[2]
            )
            pressure = (ADIABATIC - 1.0) * (cons[4, k, rows, :] - kinetic)
            sound = jnp.sqrt(ADIABATIC * pressure * inverse)
            radius = [jnp.abs(velocity[d]) + sound for d in range(3)]
            diagonal = METRIC[0] * radius[0] + METRIC[1] * radius[1] + METRIC[2] * radius[2]
            rdiag = 1.0 / diagonal
            half = (0.5 * METRIC[2]) * rdiag
            forward = (velocity[2] + radius[2]) * half
            backward = (radius[2] - velocity[2]) * half
            skew = (0.5 * METRIC[2] * COUPLING * ROOT2) * sound * rdiag
            for h in range(2):
                gain[2 * block + h, k] = tile_of(forward, h)
                gain[2 * block + h, 4 + k] = tile_of(backward, h)
                gain[2 * block + h, 8 + k] = tile_of(skew, h)
                scale[2 * block + h, k] = tile_of(rdiag, h)
            alphas.append((forward + skew, forward - skew, forward))
            betas.append((backward - skew, backward + skew, backward))

            r = [res[f, k, rows, :] for f in range(5)]
            total = r[0] + r[4]
            third = ROOT2 * r[3]
            source = [-(total + third), third - total, r[4] - r[0], -r[1], -r[2]]
            guess = [value * rdiag for value in source]
            pair = -total * rdiag
            cross = {}
            for d in range(2):
                weight = 0.5 * METRIC[d]
                plus = weight * (velocity[d] + radius[d])
                minus = weight * (velocity[d] - radius[d])
                mix = (weight * COUPLING) * sound
                outer = 2.0 * mix * guess[3 + d]
                inner = mix * pair
                extra = [outer, outer, None, None, None]
                extra[3 + d] = inner
                cross[d] = (
                    [plus * v if x is None else plus * v + x for v, x in zip(guess, extra)],
                    [minus * v if x is None else minus * v + x for v, x in zip(guess, extra)],
                )
            for e in range(5):
                n = 4 * e + k
                xp = pltpu.roll(cross[0][0][e], 1, 0)
                xm = pltpu.roll(cross[0][1][e], 7, 0)
                faces[0, block + 1, n : n + 1, :] = xp[0:1]
                faces[1, block, n : n + 1, :] = xm[7:8]
                yp, ym = cross[1][0][e], cross[1][1][e]
                base_part[n, rows, :] = (
                    source[e]
                    + jnp.where(sublane == 0, 0.0, xp)
                    + jnp.where(lane == 0, 0.0, pltpu.roll(yp, 1, 1))
                )
                up_part[n, rows, :] = (
                    jnp.where(sublane == 7, 0.0, xm)
                    + jnp.where(lane == 255, 0.0, pltpu.roll(ym, 255, 1))
                )
                edge_high = jnp.where(
                    small_lane == n, pltpu.roll(tile_of(yp, 1), (n + 1) % 128, 1), edge_high
                )
                edge_low = jnp.where(small_lane == n, pltpu.roll(tile_of(ym, 0), n, 1), edge_low)
        ys[0, rows, :] = edge_high
        ys[1, rows, :] = edge_low

        coefs = [None] * NCOEF
        for c in range(3):
            a = [alphas[k][c] for k in range(DEPTH)]
            b = [betas[k][c] for k in range(DEPTH)]
            lead = [None, a[0], a[0] * a[1], a[0] * a[1] * a[2]]
            trail = [None] * DEPTH
            trail[2] = b[3]
            trail[1] = b[3] * b[2]
            trail[0] = trail[1] * b[1]
            reply = [None] * DEPTH
            reply[3] = lead[3]
            reply[2] = lead[2] + b[3] * reply[3]
            reply[1] = lead[1] + b[2] * reply[2]
            reply[0] = 1.0 + b[1] * reply[1]
            coefs[c] = lead[3] * a[3]
            coefs[3 + c] = trail[0] * b[0]
            coefs[6 + c] = reply[0] * b[0]
            for h in range(2):
                for k in range(DEPTH):
                    pull[2 * block + h, 4 * c + k] = tile_of(reply[k], h)
                    if k < 3:
                        pull[2 * block + h, 12 + 3 * c + k] = tile_of(trail[k], h)
        for h in range(2):
            for j in range(NCOEF):
                coef_out[2 * block + h, j] = tile_of(coefs[j], h)

        @pl.when(step == 5)
        def _():
            await_plane()
            lax.fori_loop(0, step, first_send, 0)

        @pl.when(step >= 5)
        def _():
            first_send(step, 0)

        return carry

    lax.fori_loop(0, blocks, first_pass, 0)

    odd = lax.rem(me, 2)

    @pl.when(odd == 1)
    def _():
        coef_copy(me - 1, me).start()

    faces[gx, blocks * gx] = jnp.zeros((24, 256), jnp.float32)
    face = pltpu.make_async_remote_copy(
        src_ref=faces.at[gx, blocks * (1 - gx)], dst_ref=faces.at[gx, blocks * gx],
        send_sem=halo_ssem.at[0], recv_sem=halo_rsem.at[0],
        device_id={"gx": 1 - gx}, device_id_type=MESH,
    )
    face.start()
    await_neighbours()
    high = pltpu.make_async_remote_copy(
        src_ref=ys.at[0], dst_ref=yr.at[0], send_sem=halo_ssem.at[1], recv_sem=halo_rsem.at[1],
        device_id={"gy": above}, device_id_type=MESH,
    )
    high.start()
    low = pltpu.make_async_remote_copy(
        src_ref=ys.at[1], dst_ref=yr.at[1], send_sem=halo_ssem.at[2], recv_sem=halo_rsem.at[2],
        device_id={"gy": below}, device_id_type=MESH,
    )
    low.start()
    face.wait()
    high.wait()
    low.wait()

    def second_pass(group, step, carry):
        block = first_block(step)
        rows = pl.ds(pl.multiple_of(8 * block, 8), 8)
        left = jnp.where(gy > 0, yr[0, rows, :], 0.0)
        right = jnp.where(gy < gy_count - 1, yr[1, rows, :], 0.0)
        for place, e in enumerate(GROUPS[group]):
            base, side = [], []
            for k in range(DEPTH):
                n = 4 * e + k
                full = base_part[n, rows, :] + jnp.where(sublane == 0, faces[0, block, n : n + 1, :], 0.0)
                incoming = jnp.where(small_lane == 0, pltpu.roll(left, (128 - n) % 128, 1), 0.0)
                base.append((tile_of(full, 0) + incoming, tile_of(full, 1)))
                full = up_part[n, rows, :] + jnp.where(sublane == 7, faces[1, block + 1, n : n + 1, :], 0.0)
                incoming = jnp.where(small_lane == 127, pltpu.roll(right, 127 - n, 1), 0.0)
                side.append((tile_of(full, 0), tile_of(full, 1) + incoming))
            for h in range(2):
                tile = 2 * block + h
                f = [gain[tile, k] for k in range(DEPTH)]
                b = [gain[tile, 4 + k] for k in range(DEPTH)]
                if CLASS[e] != 2:
                    s = [gain[tile, 8 + k] for k in range(DEPTH)]
                    sign = 1.0 if CLASS[e] == 0 else -1.0
                    f = [x + sign * y for x, y in zip(f, s)]
                    b = [x - sign * y for x, y in zip(b, s)]
                lower = [base[0][h]]
                for k in range(1, DEPTH):
                    lower.append(base[k][h] + f[k - 1] * lower[k - 1])
                term_out[tile, START[group] + place] = f[3] * lower[3]
                upper = lower[3] - side[3][h]
                part[tile, 4 * e + 3] = upper
                for k in (2, 1, 0):
                    upper = lower[k] - side[k][h] + b[k + 1] * upper
                    part[tile, 4 * e + k] = upper
                term_out[tile, START[group] + SIZE[group] // 2 + place] = b[0] * upper
        for h in range(2):
            tile = 2 * block + h

            @pl.when((tile != me) & ((step > 0) | (tile > me)))
            def _():
                term_copy(group, tile, me).start()

        return carry

    for group in range(2):
        lax.fori_loop(0, blocks, functools.partial(second_pass, group), 0)

        @pl.when(odd == 1)
        def _():
            term_copy(group, me - 1, me).start()


    for j in range(NCOEF):
        coef_in[me, j] = coef_out[me, j]
    for j in range(NTERM):
        term_in[me, j] = term_out[me, j]

    def go_up(group, section, carry):
        nxt = []
        for place, e in enumerate(GROUPS[group]):
            j = START[group] + place
            link_out[section, j] = carry[place]
            nxt.append(coef_in[section, CLASS[e]] * carry[place] + term_in[section, j])
        return tuple(nxt)

    def go_down(group, step, carry):
        section = sections - 1 - step
        nxt = []
        for place, e in enumerate(GROUPS[group]):
            low = START[group] + place
            high = low + SIZE[group] // 2
            link_out[section, high] = carry[place]
            nxt.append(
                coef_in[section, 3 + CLASS[e]] * carry[place]
                + (term_in[section, high] + coef_in[section, 6 + CLASS[e]] * link_out[section, low])
            )
        return tuple(nxt)

    def give_back(group, step, carry):
        link_copy(group, lax.rem(me + step, sections), me).start()
        return carry

    coef_all().wait_recv()
    zero = jnp.zeros((8, 128), jnp.float32)
    for group in range(2):
        count = len(GROUPS[group])
        term_all(group).wait_recv()
        lax.fori_loop(0, sections, functools.partial(go_up, group), (zero,) * count, unroll=True)
        lax.fori_loop(0, sections, functools.partial(go_down, group), (zero,) * count, unroll=True)
        lax.fori_loop(1, sections, functools.partial(give_back, group), 0)
    for j in range(NTERM):
        link_in[me, j] = link_out[me, j]
    coef_all().wait_send()
    for group in range(2):
        term_all(group).wait_send()

    def solved(tile, k, e):
        c = CLASS[e]
        group = 0 if c == 2 else 1
        low = START[group] + GROUPS[group].index(e)
        high = low + SIZE[group] // 2
        v = part[tile, 4 * e + k] + pull[tile, 4 * c + k] * link_in[tile, low]
        if k < 3:
            return v + pull[tile, 12 + 3 * c + k] * link_in[tile, high]
        return v + link_in[tile, high]

    def last_pass(group, step, carry):
        tile = lax.rem(me - step + sections, sections)
        rows = pl.ds(pl.multiple_of(8 * (tile // 2), 8), 8)
        columns = pl.ds(pl.multiple_of(128 * lax.rem(tile, 2), 128), 128)

        @pl.when(step > 0)
        def _():
            link_copy(group, tile, tile).wait_recv()

        for k in range(DEPTH):
            rdiag = scale[tile, k]
            if group == 0:
                halfway = 0.5 * solved(tile, k, 2)
                out[0, k, rows, columns] = halfway * rdiag
                out[1, k, rows, columns] = solved(tile, k, 3) * rdiag
                out[2, k, rows, columns] = solved(tile, k, 4) * rdiag
            else:
                p, q = solved(tile, k, 0), solved(tile, k, 1)
                mean = 0.25 * (p + q) * rdiag
                halfway = out[0, k, rows, columns]
                out[0, k, rows, columns] = mean + halfway
                out[3, k, rows, columns] = (0.5 / ROOT2) * (p - q) * rdiag
                out[4, k, rows, columns] = mean - halfway
        return carry

    for group in range(2):
        lax.fori_loop(0, sections, functools.partial(last_pass, group), 0)

    for group in range(2):
        link_sent(group).wait_send()


def per_device(sections, gy_count, conserved, residual):
    rows, columns = conserved.shape[2], conserved.shape[3]
    blocks = rows // 8
    f32 = jnp.float32
    vmem = lambda *shape: pltpu.VMEM(shape, f32)
    dma = pltpu.SemaphoreType.DMA
    return pl.pallas_call(
        functools.partial(sweep_kernel, sections, gy_count, blocks),
        out_shape=pltpu.VMEM(conserved.shape, f32),
        in_specs=[pl.BlockSpec(memory_space=pltpu.HBM)] * 2,
        out_specs=pl.BlockSpec(memory_space=pltpu.VMEM),
        scratch_shapes=[
            vmem(*conserved.shape),
            vmem(*residual.shape),
            vmem(sections, 12, 8, 128),
            vmem(20, rows, columns),
            vmem(20, rows, columns),
            vmem(2, blocks + 1, 24, columns),
            vmem(sections, 21, 8, 128),
            vmem(sections, 20, 8, 128),
            vmem(sections, 4, 8, 128),
            vmem(sections, NCOEF, 8, 128),
            vmem(sections, NCOEF, 8, 128),
            vmem(sections, NTERM, 8, 128),
            vmem(sections, NTERM, 8, 128),
            vmem(sections, NTERM, 8, 128),
            vmem(sections, NTERM, 8, 128),
            vmem(2, rows, 128),
            vmem(2, rows, 128),
            dma((2, blocks)),
            dma(()),
            dma(()),
            dma((2,)),
            dma((2,)),
            dma((2,)),
            dma((2, sections)),
            dma((3,)),
            dma((3,)),
            pltpu.SemaphoreType.REGULAR,
            pltpu.SemaphoreType.REGULAR,
        ],
        compiler_params=pltpu.CompilerParams(
            collective_id=0, has_side_effects=True, vmem_limit_bytes=54 << 20
        ),
    )(conserved, residual)


def solution(mesh):
    spec = P(None, "gz", "gx", "gy")
    return jax.shard_map(
        functools.partial(per_device, mesh.shape["gz"], mesh.shape["gy"]),
        mesh=mesh, in_specs=(spec, spec), out_specs=spec, check_vma=False,
    )
```
